32 devices in a mesh: img: 8 (over z, core), pos: 4 (over y, x).
Axes of the slice: x: 2, y: 2, z: 4, core: 2. Of those that a mesh axis runs over, the one named last changes fastest.
Arguments:
- section_one: bfloat16 [64, 28, 28, 64], P(('img', 'pos')), may hold values from -6 to 6
- section_two: bfloat16 [64, 14, 14, 128], P(('img', 'pos')), may hold values from -6 to 6
- section_three: bfloat16 [64, 7, 7, 256], P(('img', 'pos')), may hold values from -6 to 6
- weight_one: bfloat16 [3, 3, 64, 64], replicated, may hold values from -0.25 to 0.25
- weight_two: bfloat16 [3, 3, 128, 128], replicated, may hold values from -0.1875 to 0.1875
- weight_three: bfloat16 [3, 3, 256, 256], replicated, may hold values from -0.125 to 0.125
- gain_one: float32 [64], replicated, may hold values from 0.25 to 1.75
- gain_two: float32 [128], replicated, may hold values from 0.25 to 1.75
- gain_three: float32 [256], replicated, may hold values from 0.25 to 1.75
- bias_one: float32 [64], replicated, may hold values from -3 to 3
- bias_two: float32 [128], replicated, may hold values from -3 to 3
- bias_three: float32 [256], replicated, may hold values from -3 to 3
- channel_index: int32 [100], replicated, may hold values from 0 to 447, as said below
- valid_count: int32 [8, 4], P('img', 'pos'), may hold values from 1 to 2, as said below
Outputs:
- mean: float32 [100, 784], P(None, 'pos')
- covariance: float32 [784, 10000], P('pos')
The draws below stay inside these ranges and needn't reach their ends.
Inputs may be any that keep to these rules, and one draw needn't show every extreme that they name: `channel_index`: 100 distinct channel numbers; 0 and 447 are always among them. `valid_count`: A device's valid images are its first slots. Every draw has a device with 2 valid images and one with 1.
All inputs are finite; a program needn't handle non-finite values.
Results may differ from the reference program's by a relative error of at most 0.0022.
Values may be sent and summed in bfloat16 or wider, within the bound.
No kernel may reach another device: no remote copies, remote signals or barrier semaphores. Data moves between devices by JAX's collectives and lax.ppermute only.
A program may use at most 128 MiB of HBM per device.

```python
import jax
import jax.numpy as jnp
from jax import lax

C1 = 64
C2 = 128
C3 = 256
CH = 448
K = 100
H1 = 28
H2 = 14
H3 = 7
POSITIONS = 784
IMG_DEV = 2
GROUPS = 8
OWNERS = 4
IMAGES = 64


def draw_channel_index(key, part):
    pick_key, order_key = jax.random.split(key)
    inner = jax.random.permutation(pick_key, CH - 2)[:K - 2] + 1
    chosen = jnp.concatenate([jnp.array([0, CH - 1], jnp.int32), inner.astype(jnp.int32)])
    return chosen[jax.random.permutation(order_key, K)].astype(jnp.int32)


def draw_valid_count(key, part):
    level_key, noise_key, place_key, other_key = jax.random.split(key, 4)
    level = jax.random.randint(level_key, (GROUPS, 1), 1, IMG_DEV + 1)
    noise = jax.random.randint(noise_key, (GROUPS, OWNERS), -1, 2)
    counts = jnp.clip(level + noise, 1, IMG_DEV).reshape(-1)
    cells = GROUPS * OWNERS
    full_at = jax.random.randint(place_key, (), 0, cells)
    low_at = (full_at + 1 + jax.random.randint(other_key, (), 0, cells - 1)) % cells
    counts = counts.at[full_at].set(IMG_DEV).at[low_at].set(1)
    return counts.reshape(GROUPS, OWNERS).astype(jnp.int32)


def block_levels(rng, extent, shards, least, top_value):
    def one(dim, parts):
        draws = jax.random.uniform(jax.random.fold_in(jax.random.fold_in(rng, 6), dim), (parts,), jnp.float32, least / len(shards), top_value / len(shards))
        return jnp.repeat(jnp.exp(draws), extent[dim] // parts).reshape((-1,) + (1,) * (len(extent) - dim - 1))

    level = one(*shards[0])
    for cut in shards[1:]:
        level = level * one(*cut)
    return level


def normal_values(stream_key, shape, spread, limit, shards=(), held_as=jnp.bfloat16):
    drawn = jax.random.normal(stream_key, shape, jnp.float32) * spread
    if len(shards) > 0:
        drawn = block_levels(stream_key, shape, shards, -0.22, 0.18) * drawn
    return jnp.clip(drawn, min=-limit, max=limit).astype(held_as)


def setup_inputs(seed: int = 0) -> dict:
    arg_keys = jax.random.split(jax.random.key(seed), 15)
    return {
        "section_one": normal_values(arg_keys[0], (IMAGES, H1, H1, C1), 1.0, 6.0, ((0, 32),)),
        "section_two": normal_values(arg_keys[1], (IMAGES, H2, H2, C2), 1.0, 6.0, ((0, 32),)),
        "section_three": normal_values(arg_keys[2], (IMAGES, H3, H3, C3), 1.0, 6.0, ((0, 32),)),
        "weight_one": normal_values(arg_keys[3], (3, 3, C1, C1), (9 * C1) ** -0.5, 0.25),
        "weight_two": normal_values(arg_keys[4], (3, 3, C2, C2), (9 * C2) ** -0.5, 0.1875),
        "weight_three": normal_values(arg_keys[5], (3, 3, C3, C3), (9 * C3) ** -0.5, 0.125),
        "gain_one": jnp.clip(1.0 + 0.15 * jax.random.normal(arg_keys[6], (C1,), jnp.float32), 0.25, 1.75),
        "gain_two": jnp.clip(1.0 + 0.15 * jax.random.normal(arg_keys[7], (C2,), jnp.float32), 0.25, 1.75),
        "gain_three": jnp.clip(1.0 + 0.15 * jax.random.normal(arg_keys[8], (C3,), jnp.float32), 0.25, 1.75),
        "bias_one": normal_values(arg_keys[9], (C1,), 0.5, 3.0, (), jnp.float32),
        "bias_two": normal_values(arg_keys[10], (C2,), 0.5, 3.0, (), jnp.float32),
        "bias_three": normal_values(arg_keys[11], (C3,), 0.5, 3.0, (), jnp.float32),
        "channel_index": draw_channel_index(jax.random.fold_in(arg_keys[14], 71), 0),
        "valid_count": draw_valid_count(jax.random.fold_in(arg_keys[14], 71), 0),
    }


def section_out(images, weight, gain, bias):
    conv = lax.conv_general_dilated(images.astype(jnp.float32), weight.astype(jnp.float32), (1, 1), "SAME", dimension_numbers=("NHWC", "HWIO", "NHWC"), precision=lax.Precision.HIGHEST)
    return jax.nn.relu(conv * gain + bias).astype(jnp.bfloat16)


def pick_channels(section, offset, width, channel_index):
    table = (channel_index[None, :] - offset == jnp.arange(width, dtype=jnp.int32)[:, None]).astype(jnp.float32)
    return jnp.einsum("ihwc,ck->ikhw", section.astype(jnp.float32), table).astype(jnp.bfloat16)


def widen(picked, factor):
    return jnp.repeat(jnp.repeat(picked, factor, axis=2), factor, axis=3)


def reference(section_one, section_two, section_three, weight_one, weight_two, weight_three, gain_one, gain_two, gain_three, bias_one, bias_two, bias_three, channel_index, valid_count):
    per_block = IMG_DEV * OWNERS
    image_ids = jnp.arange(IMAGES, dtype=jnp.int32)
    flat_counts = valid_count.reshape(-1)
    valid = (image_ids % IMG_DEV < flat_counts[image_ids // IMG_DEV]).astype(jnp.float32)
    total = jnp.sum(valid)

    def accumulate(carry, inputs):
        sums, raw = carry
        first, second, third, valid_rows = inputs
        scale = valid_rows.astype(jnp.bfloat16)[:, None, None, None]
        out_one = section_out(first, weight_one, gain_one, bias_one) * scale
        out_two = section_out(second, weight_two, gain_two, bias_two) * scale
        out_three = section_out(third, weight_three, gain_three, bias_three) * scale
        features = pick_channels(out_one, 0, C1, channel_index)
        features = features + widen(pick_channels(out_two, C1, C2, channel_index), 2)
        features = features + widen(pick_channels(out_three, C1 + C2, C3, channel_index), 4)
        values = features.reshape(per_block, K, POSITIONS).astype(jnp.float32)
        sums = sums + jnp.sum(values, axis=0)
        raw = raw + jnp.einsum("ikp,ilp->pkl", values, values).reshape(POSITIONS, K * K)
        return (sums, raw), None

    inputs = (section_one.reshape(GROUPS, per_block, H1, H1, C1), section_two.reshape(GROUPS, per_block, H2, H2, C2), section_three.reshape(GROUPS, per_block, H3, H3, C3), valid.reshape(GROUPS, per_block))
    start = (jnp.zeros((K, POSITIONS), jnp.float32), jnp.zeros((POSITIONS, K * K), jnp.float32))
    (sums, raw), unused = lax.scan(accumulate, start, inputs)
    mean = sums / total
    turned = mean.T
    moment = raw - total * (turned[:, :, None] * turned[:, None, :]).reshape(POSITIONS, K * K)
    covariance = moment / (total - 1.0) + 0.01 * jnp.eye(K, dtype=jnp.float32).reshape(1, K * K)
    return mean, covariance
```

```python
import functools

import jax
import jax.numpy as jnp
import numpy as np
from jax import lax
from jax.experimental import pallas as pl
from jax.experimental.pallas import tpu as pltpu
from jax.sharding import PartitionSpec as P

LANES = 128
HALF = 64
PAIR = 2


def section_out(images, weight, gain, bias):
    conv = lax.conv_general_dilated(
        images,
        weight,
        (1, 1),
        "SAME",
        dimension_numbers=("NHWC", "HWIO", "NHWC"),
        preferred_element_type=jnp.float32,
    )
    return jax.nn.relu(conv * gain + bias).astype(jnp.bfloat16)


def pick_channels(section, offset, width, channel_index):
    table = (channel_index[None, :] - offset == lax.iota(jnp.int32, width)[:, None]).astype(
        jnp.bfloat16
    )
    return jnp.einsum("ihwc,ck->ikhw", section, table, preferred_element_type=jnp.float32).astype(
        jnp.bfloat16
    )


def widen(picked, factor):
    return jnp.repeat(jnp.repeat(picked, factor, axis=2), factor, axis=3)


def pair_outer(rows):
    return (rows[:, :, None] * rows[:, None, :]).reshape(
        rows.shape[0], rows.shape[1] * rows.shape[1]
    )


def product_rows(values):
    kept = values.shape[1]
    raw = jnp.einsum("ikp,ilp->pkl", values, values, preferred_element_type=jnp.float32)
    return raw.reshape(values.shape[2], kept * kept)


def plain(
    section_one,
    section_two,
    section_three,
    weight_one,
    weight_two,
    weight_three,
    gain_one,
    gain_two,
    gain_three,
    bias_one,
    bias_two,
    bias_three,
    channel_index,
    valid_count,
):
    slots = section_one.shape[0]
    side = section_one.shape[1]
    width_one = section_one.shape[3]
    width_two = section_two.shape[3]
    width_three = section_three.shape[3]
    kept = channel_index.shape[0]
    owners = lax.axis_size("pos")
    block = side * side // owners
    own_count = valid_count[0, 0]
    scale = (lax.iota(jnp.int32, slots) < own_count).astype(jnp.bfloat16)[:, None, None, None]
    out_one = section_out(section_one, weight_one, gain_one, bias_one) * scale
    out_two = section_out(section_two, weight_two, gain_two, bias_two) * scale
    out_three = section_out(section_three, weight_three, gain_three, bias_three) * scale
    features = pick_channels(out_one, 0, width_one, channel_index)
    features = features + widen(pick_channels(out_two, width_one, width_two, channel_index), 2)
    features = features + widen(
        pick_channels(out_three, width_one + width_two, width_three, channel_index), 4
    )
    shaped = features.reshape(slots, kept, owners, block)
    group = lax.psum(own_count, "pos").astype(jnp.float32)
    owned = lax.all_to_all(shaped, "pos", split_axis=2, concat_axis=0, tiled=True)[:, :, 0, :]
    values = lax.all_gather(owned, "img", axis=0, tiled=True)
    counts = lax.all_gather(group.astype(jnp.bfloat16)[None], "img", axis=0, tiled=True)
    total = jnp.sum(counts.astype(jnp.float32))
    all_sums = jnp.sum(values, axis=0, dtype=jnp.float32).T
    all_raw = product_rows(values)
    mean = all_sums / total
    moment = all_raw - total * pair_outer(mean)
    covariance = moment / (total - 1.0) + 0.01 * jnp.eye(kept, dtype=jnp.float32).reshape(
        1, kept * kept
    )
    return (mean.T, covariance)


def dot(a, b):
    return lax.dot_general(a, b, (((1,), (0,)), ((), ())), preferred_element_type=jnp.float32)


def iota(shape, dim):
    return lax.broadcasted_iota(jnp.int32, shape, dim)


def padded_index(idx_ref):
    kept = idx_ref.shape[1]
    lane = iota((1, LANES), 1)
    row = jnp.concatenate([idx_ref[...], jnp.zeros((1, LANES - kept), jnp.int32)], axis=1)
    return jnp.where(lane < kept, row, 100000 + lane).astype(jnp.float32)


def column_of(row):
    spread = jnp.broadcast_to(row, (LANES, LANES))
    diagonal = iota((LANES, LANES), 0) == iota((LANES, LANES), 1)
    return jnp.sum(jnp.where(diagonal, spread, 0.0), axis=1, keepdims=True)


def rank_row(idx_row):
    smaller = column_of(idx_row) < idx_row
    return jnp.sum(jnp.where(smaller, 1.0, 0.0), axis=0, keepdims=True)


def one_hot(mask):
    return jnp.where(mask, 1.0, 0.0).astype(jnp.bfloat16)


def features_kernel(
    dims,
    s1_ref,
    s2_ref,
    s3_ref,
    w1_ref,
    w2_ref,
    w3_ref,
    g1_ref,
    g2_ref,
    g3_ref,
    b1_ref,
    b2_ref,
    b3_ref,
    idx_ref,
    count_ref,
    p1_ref,
    p2_ref,
    p3_ref,
    up_ref,
    c1_ref,
    c2_ref,
    out_ref,
    buf1,
    buf2,
    buf3,
    wgt1,
):
    h1, h2, h3, owners, kept, group, pitch2, pitch3 = dims
    count = count_ref[0, 0]
    base2, base3 = HALF, HALF + LANES

    def keep(values, gain, bias):
        image = iota((values.shape[0], 1), 0) % PAIR
        shaped = jnp.maximum(values * gain + bias, 0.0)
        return jnp.where(image < count, shaped, 0.0).astype(jnp.bfloat16)

    index_row = padded_index(idx_ref)
    rank_col = column_of(rank_row(index_row))
    slot = iota((LANES, LANES), 1).astype(jnp.float32)
    ranked = jnp.sum(jnp.where(rank_col == slot, column_of(index_row), 0.0), axis=0, keepdims=True)
    ranked = ranked.astype(jnp.int32)
    low = jnp.concatenate([ranked[:, :HALF], ranked[:, :HALF]], axis=1)
    high = jnp.concatenate([ranked[:, HALF:], ranked[:, HALF:]], axis=1)
    both = jnp.concatenate([low, high], axis=1)
    row128, lane128 = iota((LANES, LANES), 0), iota((LANES, LANES), 1)
    same_half = (row128 // HALF) == (lane128 // HALF)
    pick1 = one_hot((low == row128 % HALF) & same_half)
    pick2 = one_hot(both == base2 + iota((LANES, 2 * LANES), 0))
    pick3 = one_hot(both == base3 + iota((2 * LANES, 2 * LANES), 0))

    rows3 = pitch3 * PAIR
    body3 = h3 * rows3
    buf3[0:rows3, :] = jnp.zeros((rows3, buf3.shape[1]), jnp.bfloat16)
    buf3[rows3 + body3 :, :] = jnp.zeros((rows3, buf3.shape[1]), jnp.bfloat16)
    third = s3_ref[...]
    width3 = third.shape[1]
    for tap in range(3):
        moved = dot(p3_ref[tap], third).astype(jnp.bfloat16)
        buf3[rows3 : rows3 + body3, tap * width3 : (tap + 1) * width3] = moved
    acc3 = None
    for dy in range(3):
        for tap in range(3):
            left = buf3[dy * rows3 : dy * rows3 + body3, tap * width3 : (tap + 1) * width3]
            term = dot(left, w3_ref[dy, tap])
            acc3 = term if acc3 is None else acc3 + term
    out3 = keep(acc3, g3_ref[...], b3_ref[...])
    chosen3 = dot(out3, pick3).astype(jnp.bfloat16)

    rows2 = pitch2 * PAIR
    body2 = h2 * rows2
    native2 = h2 * PAIR
    buf2[0:rows2, :] = jnp.zeros((rows2, buf2.shape[1]), jnp.bfloat16)
    buf2[rows2 + body2 :, :] = jnp.zeros((rows2, buf2.shape[1]), jnp.bfloat16)
    for first in range(0, h2, group):
        lines = min(group, h2 - first)
        block = s2_ref[first * native2 : (first + lines) * native2, :]
        for tap in range(3):
            moved = dot(p2_ref[tap, : lines * rows2, : lines * native2], block).astype(jnp.bfloat16)
            start = (1 + first) * rows2
            buf2[start : start + lines * rows2, tap * LANES : (tap + 1) * LANES] = moved
    acc2 = None
    for dy in range(3):
        left = buf2[dy * rows2 : dy * rows2 + body2, :]
        term = dot(left, w2_ref[dy].reshape(3 * LANES, LANES))
        acc2 = term if acc2 is None else acc2 + term
    out2 = keep(acc2, g2_ref[...], b2_ref[...])
    coarse = dot(out2, pick2) + dot(up_ref[...], chosen3)
    lane = iota((body2, 2 * LANES), 1)
    image = iota((body2, 2 * LANES), 0) % PAIR
    flag = (lane >= LANES) & (lane % HALF == kept - HALF)
    coarse = jnp.where(flag, jnp.where(image < count, 1.0, 0.0), coarse)

    zero = jnp.zeros((HALF, HALF), jnp.bfloat16)
    for dy in range(3):
        taps = [w1_ref[dy, 0], w1_ref[dy, 1], w1_ref[dy, 2]]
        wgt1[dy, 0:HALF, :] = jnp.concatenate([taps[1], taps[0]], axis=1)
        wgt1[dy, HALF : 2 * HALF, :] = jnp.concatenate([taps[2], taps[1]], axis=1)
        wgt1[dy, 2 * HALF : 3 * HALF, :] = jnp.concatenate([zero, taps[2]], axis=1)
        wgt1[dy, 3 * HALF :, :] = jnp.concatenate([taps[0], zero], axis=1)
    body1 = h1 * rows2
    native1 = h1 * PAIR
    buf1[0:rows2, :] = jnp.zeros((rows2, buf1.shape[1]), jnp.bfloat16)
    buf1[rows2 + body1 :, :] = jnp.zeros((rows2, buf1.shape[1]), jnp.bfloat16)
    for first in range(0, h1, group):
        lines = min(group, h1 - first)
        block = s1_ref[first * native1 : (first + lines) * native1, :]
        twice = jnp.concatenate([block, block], axis=1)
        lower = iota((lines * rows2, LANES), 1) < HALF
        moved = [dot(p1_ref[t, : lines * rows2, : lines * native1], twice) for t in range(4)]
        start = (1 + first) * rows2
        stop = start + lines * rows2
        buf1[start:stop, 0:LANES] = jnp.where(lower, moved[0], moved[1]).astype(jnp.bfloat16)
        buf1[start:stop, LANES:] = jnp.where(lower, moved[2], moved[3]).astype(jnp.bfloat16)
    acc1 = None
    for dy in range(3):
        term = dot(buf1[dy * rows2 : dy * rows2 + body1, :], wgt1[dy])
        acc1 = term if acc1 is None else acc1 + term
    gain1 = jnp.concatenate([g1_ref[...], g1_ref[...]], axis=1)
    bias1 = jnp.concatenate([b1_ref[...], b1_ref[...]], axis=1)
    out1 = keep(acc1, gain1, bias1)
    fine = dot(out1, pick1)
    spread = jnp.broadcast_to(
        coarse[:, :LANES].reshape(h2, 1, rows2, LANES), (h2, PAIR, rows2, LANES)
    ).reshape(body1, LANES)
    fine = (fine + spread).astype(jnp.bfloat16)
    coarse = coarse[:, LANES:].astype(jnp.bfloat16)

    lines = h1 // owners
    lower = iota((PAIR * rows2, LANES), 1) < HALF
    for owner in range(owners):
        base = owner * lines // PAIR
        wide = fine[owner * lines * rows2 : (owner + 1) * lines * rows2, :]
        front = coarse[base * rows2 : (base + PAIR) * rows2, :]
        back = coarse[(base + PAIR) * rows2 : (base + 2 * PAIR) * rows2, :]
        narrow = jnp.where(lower, front, back)
        packed = dot(c1_ref[...], wide) + dot(c2_ref[...], narrow)
        out_ref[owner] = packed.astype(jnp.bfloat16)


def merge_kernel(p_ref, a_ref, b_ref, c_ref, d_ref, out_ref):
    piece = LANES // 4
    for part in range(out_ref.shape[0] // LANES):
        rows = slice(part * piece, (part + 1) * piece)
        stack = jnp.concatenate([r[rows, :] for r in (a_ref, b_ref, c_ref, d_ref)], axis=0)
        out_ref[part * LANES : (part + 1) * LANES, :] = dot(p_ref[...], stack).astype(jnp.bfloat16)


def covariance_kernel(dims, *refs):
    shards, lines, columns, kept, depth = dims
    idx_ref = refs[0]
    shard_refs = refs[1 : 1 + shards]
    mean_ref, cov_ref = refs[1 + shards : 3 + shards]
    rows, spread, table, gram = refs[3 + shards :]
    step = pl.program_id(0)
    images = rows.shape[1]
    each = images // shards
    positions = lines * columns

    @pl.when(step == 0)
    def _():
        for j in range(shards):
            rows[:, j * each : (j + 1) * each, :] = shard_refs[j][...]
        rank = rank_row(padded_index(idx_ref)).astype(jnp.int32)
        rank2 = jnp.concatenate([rank, rank], axis=1)
        r = iota((LANES, 2 * LANES), 0)
        c = iota((LANES, 2 * LANES), 1)
        top = one_hot((rank2 == r % HALF) & (r // HALF == c // LANES))
        for half in range(2):
            table[half, 0:LANES, :] = top
            table[half, LANES:, :] = one_hot((rank2 - HALF == r % HALF) & (r // HALF == half))
        odd = (lines * lax.axis_index("pos")) % PAIR
        for line in range(lines):
            level = (line + odd) // PAIR
            left = rows[line * columns : (line + 1) * columns].reshape(columns * images, LANES)
            at = positions + (level % PAIR) * columns
            right = rows[pl.ds(at, columns)].reshape(columns * images, LANES)
            both = jnp.concatenate([left, right], axis=1)
            wide = dot(both, table[level // PAIR]).astype(jnp.bfloat16)
            spread[line * columns : (line + 1) * columns] = wide.reshape(
                columns, images, 2 * LANES
            )
        tail = spread.shape[0] - positions
        if tail:
            spread[positions:] = jnp.zeros((tail, images, 2 * LANES), jnp.bfloat16)

    for t in range(4):
        pair = spread[step * 4 + t]
        for side in range(PAIR):
            x = pair[:, side * LANES : (side + 1) * LANES]
            product = lax.dot_general(
                x, x, (((0,), (0,)), ((), ())), preferred_element_type=jnp.float32
            )
            at = (t * PAIR + side) * depth
            gram[at : at + depth, :] = product[:depth, :]
    sums = gram[pl.ds(kept, 8, stride=depth), :]
    total = sums[:, kept : kept + 1]
    mean = sums / total
    mean_ref[...] = mean[:, :kept]
    inverse = jnp.broadcast_to(1.0 / (total - 1.0), (8, LANES))
    lane = iota((8, LANES), 1)
    for k in range(kept):
        raw = gram[pl.ds(k, 8, stride=depth), :]
        value = (raw - mean[:, k : k + 1] * sums) * inverse
        value = value + jnp.where(lane == k, 0.01, 0.0)
        cov_ref[:, k * kept : (k + 1) * kept] = value[:, :kept]


def shift_tables(h1, h2, h3, owners, group, pitch2, pitch3):
    rows2 = pitch2 * PAIR
    p1 = np.zeros((4, group * rows2, group * h1 * PAIR), np.float32)
    p2 = np.zeros((3, group * rows2, group * h2 * PAIR), np.float32)
    for y in range(group):
        for x in range(h2):
            for i in range(PAIR):
                to = y * rows2 + x * PAIR + i
                for t, source in enumerate((2 * x, 2 * x + 1, 2 * x + 2, 2 * x - 1)):
                    if 0 <= source < h1:
                        p1[t, to, (y * h1 + source) * PAIR + i] = 1
                for t in range(3):
                    if 0 <= x + t - 1 < h2:
                        p2[t, to, (y * h2 + x + t - 1) * PAIR + i] = 1
    p3 = np.zeros((3, h3 * pitch3 * PAIR, h3 * h3 * PAIR), np.float32)
    for y in range(h3):
        for x in range(h3):
            for i in range(PAIR):
                for t in range(3):
                    if 0 <= x + t - 1 < h3:
                        p3[t, (y * pitch3 + x) * PAIR + i, (y * h3 + x + t - 1) * PAIR + i] = 1
    up = np.zeros((h2 * rows2, h3 * pitch3 * PAIR), np.float32)
    for y in range(h2):
        for x in range(h2):
            for i in range(PAIR):
                up[y * rows2 + x * PAIR + i, ((y // 2) * pitch3 + x // 2) * PAIR + i] = 1
    lines = h1 // owners
    packed = pack_rows(h1, owners)
    c1 = np.zeros((packed, lines * rows2), np.float32)
    c2 = np.zeros((packed, PAIR * rows2), np.float32)
    for x in range(h2):
        for i in range(PAIR):
            for y in range(lines):
                c1[(y * h2 + x) * PAIR + i, y * rows2 + x * PAIR + i] = 1
            for y in range(PAIR):
                c2[((lines + y) * h2 + x) * PAIR + i, y * rows2 + x * PAIR + i] = 1
    return [jnp.asarray(a, jnp.bfloat16) for a in (p1, p2, p3, up, c1, c2)]


def pack_rows(h1, owners):
    lines = h1 // owners
    rows = (lines + PAIR) * (h1 // 2) * PAIR
    return -(-rows // 32) * 32


def merge_table():
    table = np.zeros((LANES, LANES), np.float32)
    for r in range(16):
        for s in range(4):
            for i in range(PAIR):
                table[r * 8 + s * PAIR + i, s * 32 + r * PAIR + i] = 1
    return jnp.asarray(table, jnp.bfloat16)


def whole(array):
    zeros = (0,) * array.ndim
    return pl.BlockSpec(array.shape, lambda g: zeros, pipeline_mode=pl.Buffered(1))


def packed_path(
    section_one,
    section_two,
    section_three,
    weight_one,
    weight_two,
    weight_three,
    gain_one,
    gain_two,
    gain_three,
    bias_one,
    bias_two,
    bias_three,
    channel_index,
    valid_count,
):
    slots, h1 = section_one.shape[:2]
    h2, h3 = section_two.shape[1], section_three.shape[1]
    c1, c2, c3 = section_one.shape[3], section_two.shape[3], section_three.shape[3]
    kept = channel_index.shape[0]
    owners = lax.axis_size("pos")
    groups = lax.axis_size("img")
    group, pitch2, pitch3 = 4, 16, 8
    tables = shift_tables(h1, h2, h3, owners, group, pitch2, pitch3)
    packed = pack_rows(h1, owners)
    rows2, rows3 = pitch2 * PAIR, pitch3 * PAIR

    def flat(section):
        return jnp.transpose(section, (1, 2, 0, 3)).reshape(-1, section.shape[3])

    index = channel_index.reshape(1, kept)
    smem = pl.BlockSpec(memory_space=pltpu.SMEM)
    operands = [
        flat(section_one),
        flat(section_two),
        flat(section_three),
        weight_one,
        weight_two,
        weight_three,
        gain_one.reshape(1, c1),
        gain_two.reshape(1, c2),
        gain_three.reshape(1, c3),
        bias_one.reshape(1, c1),
        bias_two.reshape(1, c2),
        bias_three.reshape(1, c3),
        index,
    ]
    packs_shape = jax.ShapeDtypeStruct((owners, packed, LANES), jnp.bfloat16)
    packs = pl.pallas_call(
        functools.partial(
            features_kernel, (h1, h2, h3, owners, kept, group, pitch2, pitch3)
        ),
        out_shape=packs_shape,
        grid=(1,),
        in_specs=[whole(a) for a in operands] + [smem] + [whole(a) for a in tables],
        out_specs=whole(packs_shape),
        scratch_shapes=[
            pltpu.VMEM(((h1 + 2) * rows2, 2 * LANES), jnp.bfloat16),
            pltpu.VMEM(((h2 + 2) * rows2, 3 * LANES), jnp.bfloat16),
            pltpu.VMEM(((h3 + 2) * rows3, 3 * c3), jnp.bfloat16),
            pltpu.VMEM((3, 2 * LANES, LANES), jnp.bfloat16),
        ],
        name="features",
    )(*operands, valid_count, *tables)

    me = lax.axis_index("pos")
    parts = [lax.dynamic_index_in_dim(packs, me, 0, keepdims=False)]
    for k in range(1, owners):
        pairs = [(i, i ^ k) for i in range(owners)]
        piece = lax.dynamic_index_in_dim(packs, me ^ k, 0, keepdims=False)
        parts.append(lax.ppermute(piece, "pos", pairs))
    merged_shape = jax.ShapeDtypeStruct((packed * owners, LANES), jnp.bfloat16)
    merging = [merge_table(), *parts]
    merged = pl.pallas_call(
        merge_kernel,
        out_shape=merged_shape,
        grid=(1,),
        in_specs=[whole(a) for a in merging],
        out_specs=whole(merged_shape),
        name="merge",
    )(*merging)

    levels = groups // PAIR
    shards = [merged]
    turns = sorted(range(1, levels), key=lambda t: (min(t, levels - t), t))
    for turn in turns:
        pairs = [
            (z * PAIR + c, ((z + turn) % levels) * PAIR + c)
            for z in range(levels)
            for c in range(PAIR)
        ]
        shards.append(lax.ppermute(merged, "img", pairs))
    swap = [(i, i ^ 1) for i in range(groups)]
    shards = shards + [lax.ppermute(s, "img", swap) for s in shards]

    lines, columns = h1 // owners, h2
    block = lines * h1
    each = owners * slots
    images = each * len(shards)
    shards = [s.reshape(packed // PAIR, each, LANES) for s in shards]
    steps = -(-block // 8)
    depth = -(-(kept + 1) // 8) * 8
    once = lambda shape: pl.BlockSpec(
        shape, lambda g: (0,) * len(shape), pipeline_mode=pl.Buffered(1)
    )
    mean, covariance = pl.pallas_call(
        functools.partial(covariance_kernel, (len(shards), lines, columns, kept, depth)),
        out_shape=(
            jax.ShapeDtypeStruct((block, kept), jnp.float32),
            jax.ShapeDtypeStruct((block, kept * kept), jnp.float32),
        ),
        grid=(steps,),
        in_specs=[once((1, kept))] + [once((packed // PAIR, each, LANES))] * len(shards),
        out_specs=(
            pl.BlockSpec((8, kept), lambda g: (g, 0)),
            pl.BlockSpec((8, kept * kept), lambda g: (g, 0)),
        ),
        scratch_shapes=[
            pltpu.VMEM((packed // PAIR, images, LANES), jnp.bfloat16),
            pltpu.VMEM((steps * 4, images, 2 * LANES), jnp.bfloat16),
            pltpu.VMEM((2, 2 * LANES, 2 * LANES), jnp.bfloat16),
            pltpu.VMEM((8 * depth, LANES), jnp.float32),
        ],
        name="covariance",
    )(index, *shards)
    return mean.T, covariance


def suits(mesh, section_one, section_two, section_three, channel_index):
    owners, groups = mesh.shape["pos"], mesh.shape["img"]
    devices = owners * groups
    images, h1, _, c1 = section_one.shape
    h2, c2 = section_two.shape[1], section_two.shape[3]
    h3, c3 = section_three.shape[1], section_three.shape[3]
    kept = channel_index.shape[0]
    lines = h1 // owners
    return (
        images == PAIR * devices
        and owners == 4
        and groups % PAIR == 0
        and h1 % owners == 0
        and h1 == 2 * h2 == 4 * h3
        and h2 <= 16
        and h3 <= 8
        and (c1, c2, c3) == (HALF, LANES, 2 * LANES)
        and HALF <= kept < LANES
        and kept - HALF < HALF
        and lines == 7
    )


def solution(mesh):
    in_specs = (
        P(("img", "pos"), None, None, None),
        P(("img", "pos"), None, None, None),
        P(("img", "pos"), None, None, None),
        P(),
        P(),
        P(),
        P(),
        P(),
        P(),
        P(),
        P(),
        P(),
        P(),
        P("img", "pos"),
    )

    def run(*arrays):
        chosen = suits(mesh, arrays[0], arrays[1], arrays[2], arrays[12])
        return jax.shard_map(
            packed_path if chosen else plain,
            mesh=mesh,
            in_specs=in_specs,
            out_specs=(P(None, "pos"), P("pos", None)),
            check_vma=False,
        )(*arrays)

    return run
```

```python
import functools

import jax
import jax.numpy as jnp
import numpy as np
from jax import lax
from jax.experimental import pallas as pl
from jax.experimental.pallas import tpu as pltpu
from jax.sharding import PartitionSpec as P

LANES = 128
HALF = 64
PAIR = 2


def section_out(images, weight, gain, bias):
    conv = lax.conv_general_dilated(
        images,
        weight,
        (1, 1),
        "SAME",
        dimension_numbers=("NHWC", "HWIO", "NHWC"),
        preferred_element_type=jnp.float32,
    )
    return jax.nn.relu(conv * gain + bias).astype(jnp.bfloat16)


def pick_channels(section, offset, width, channel_index):
    table = (channel_index[None, :] - offset == lax.iota(jnp.int32, width)[:, None]).astype(
        jnp.bfloat16
    )
    return jnp.einsum("ihwc,ck->ikhw", section, table, preferred_element_type=jnp.float32).astype(
        jnp.bfloat16
    )


def widen(picked, factor):
    return jnp.repeat(jnp.repeat(picked, factor, axis=2), factor, axis=3)


def pair_outer(rows):
    return (rows[:, :, None] * rows[:, None, :]).reshape(
        rows.shape[0], rows.shape[1] * rows.shape[1]
    )


def product_rows(values):
    kept = values.shape[1]
    raw = jnp.einsum("ikp,ilp->pkl", values, values, preferred_element_type=jnp.float32)
    return raw.reshape(values.shape[2], kept * kept)


def plain(
    section_one,
    section_two,
    section_three,
    weight_one,
    weight_two,
    weight_three,
    gain_one,
    gain_two,
    gain_three,
    bias_one,
    bias_two,
    bias_three,
    channel_index,
    valid_count,
):
    slots = section_one.shape[0]
    side = section_one.shape[1]
    width_one = section_one.shape[3]
    width_two = section_two.shape[3]
    width_three = section_three.shape[3]
    kept = channel_index.shape[0]
    owners = lax.axis_size("pos")
    block = side * side // owners
    own_count = valid_count[0, 0]
    scale = (lax.iota(jnp.int32, slots) < own_count).astype(jnp.bfloat16)[:, None, None, None]
    out_one = section_out(section_one, weight_one, gain_one, bias_one) * scale
    out_two = section_out(section_two, weight_two, gain_two, bias_two) * scale
    out_three = section_out(section_three, weight_three, gain_three, bias_three) * scale
    features = pick_channels(out_one, 0, width_one, channel_index)
    features = features + widen(pick_channels(out_two, width_one, width_two, channel_index), 2)
    features = features + widen(
        pick_channels(out_three, width_one + width_two, width_three, channel_index), 4
    )
    shaped = features.reshape(slots, kept, owners, block)
    group = lax.psum(own_count, "pos").astype(jnp.float32)
    owned = lax.all_to_all(shaped, "pos", split_axis=2, concat_axis=0, tiled=True)[:, :, 0, :]
    values = lax.all_gather(owned, "img", axis=0, tiled=True)
    counts = lax.all_gather(group.astype(jnp.bfloat16)[None], "img", axis=0, tiled=True)
    total = jnp.sum(counts.astype(jnp.float32))
    all_sums = jnp.sum(values, axis=0, dtype=jnp.float32).T
    all_raw = product_rows(values)
    mean = all_sums / total
    moment = all_raw - total * pair_outer(mean)
    covariance = moment / (total - 1.0) + 0.01 * jnp.eye(kept, dtype=jnp.float32).reshape(
        1, kept * kept
    )
    return (mean.T, covariance)


def dot(a, b):
    return lax.dot_general(a, b, (((1,), (0,)), ((), ())), preferred_element_type=jnp.float32)


def iota(shape, dim):
    return lax.broadcasted_iota(jnp.int32, shape, dim)


def padded_index(idx_ref):
    kept = idx_ref.shape[1]
    lane = iota((1, LANES), 1)
    row = jnp.concatenate([idx_ref[...], jnp.zeros((1, LANES - kept), jnp.int32)], axis=1)
    return jnp.where(lane < kept, row, 100000 + lane).astype(jnp.float32)


def column_of(row):
    spread = jnp.broadcast_to(row, (LANES, LANES))
    diagonal = iota((LANES, LANES), 0) == iota((LANES, LANES), 1)
    return jnp.sum(jnp.where(diagonal, spread, 0.0), axis=1, keepdims=True)


def rank_row(idx_row):
    smaller = column_of(idx_row) < idx_row
    return jnp.sum(jnp.where(smaller, 1.0, 0.0), axis=0, keepdims=True)


def one_hot(mask):
    return jnp.where(mask, 1.0, 0.0).astype(jnp.bfloat16)


def pieces(values):
    found = []
    for _ in range(3):
        piece = values.astype(jnp.bfloat16).astype(jnp.float32)
        found.append(piece)
        values = values - piece
    return found


def features_kernel(
    dims,
    s1_ref,
    s2_ref,
    s3_ref,
    w1_ref,
    w2_ref,
    w3_ref,
    g1_ref,
    g2_ref,
    g3_ref,
    b1_ref,
    b2_ref,
    b3_ref,
    idx_ref,
    count_ref,
    p1_ref,
    p2_ref,
    p3_ref,
    up_ref,
    c1_ref,
    c2_ref,
    out_ref,
    buf1,
    buf2,
    buf3,
    wgt1,
):
    h1, h2, h3, owners, kept, group, pitch2, pitch3 = dims
    count = count_ref[0, 0]
    base2, base3 = HALF, HALF + LANES

    def keep(values, gain, bias):
        image = iota((values.shape[0], 1), 0) % PAIR
        shaped = jnp.maximum(values * gain + bias, 0.0)
        return jnp.where(image < count, shaped, 0.0).astype(jnp.bfloat16)

    index_row = padded_index(idx_ref)
    rank_col = column_of(rank_row(index_row))
    slot = iota((LANES, LANES), 1).astype(jnp.float32)
    ranked = jnp.sum(jnp.where(rank_col == slot, column_of(index_row), 0.0), axis=0, keepdims=True)
    ranked = ranked.astype(jnp.int32)
    low = jnp.concatenate([ranked[:, :HALF], ranked[:, :HALF]], axis=1)
    high = jnp.concatenate([ranked[:, HALF:], ranked[:, HALF:]], axis=1)
    both = jnp.concatenate([low, high], axis=1)
    row128, lane128 = iota((LANES, LANES), 0), iota((LANES, LANES), 1)
    same_half = (row128 // HALF) == (lane128 // HALF)
    pick1 = one_hot((low == row128 % HALF) & same_half)
    pick2 = one_hot(both == base2 + iota((LANES, 2 * LANES), 0))
    pick3 = one_hot(both == base3 + iota((2 * LANES, 2 * LANES), 0))

    rows3 = pitch3 * PAIR
    body3 = h3 * rows3
    buf3[0:rows3, :] = jnp.zeros((rows3, buf3.shape[1]), jnp.bfloat16)
    buf3[rows3 + body3 :, :] = jnp.zeros((rows3, buf3.shape[1]), jnp.bfloat16)
    third = s3_ref[...]
    width3 = third.shape[1]
    for tap in range(3):
        moved = dot(p3_ref[tap], third).astype(jnp.bfloat16)
        buf3[rows3 : rows3 + body3, tap * width3 : (tap + 1) * width3] = moved
    acc3 = None
    for dy in range(3):
        for tap in range(3):
            left = buf3[dy * rows3 : dy * rows3 + body3, tap * width3 : (tap + 1) * width3]
            term = dot(left, w3_ref[dy, tap])
            acc3 = term if acc3 is None else acc3 + term
    out3 = keep(acc3, g3_ref[...], b3_ref[...])
    chosen3 = dot(out3, pick3).astype(jnp.bfloat16)

    rows2 = pitch2 * PAIR
    body2 = h2 * rows2
    native2 = h2 * PAIR
    buf2[0:rows2, :] = jnp.zeros((rows2, buf2.shape[1]), jnp.bfloat16)
    buf2[rows2 + body2 :, :] = jnp.zeros((rows2, buf2.shape[1]), jnp.bfloat16)
    for first in range(0, h2, group):
        lines = min(group, h2 - first)
        block = s2_ref[first * native2 : (first + lines) * native2, :]
        for tap in range(3):
            moved = dot(p2_ref[tap, : lines * rows2, : lines * native2], block).astype(jnp.bfloat16)
            start = (1 + first) * rows2
            buf2[start : start + lines * rows2, tap * LANES : (tap + 1) * LANES] = moved
    acc2 = None
    for dy in range(3):
        left = buf2[dy * rows2 : dy * rows2 + body2, :]
        term = dot(left, w2_ref[dy].reshape(3 * LANES, LANES))
        acc2 = term if acc2 is None else acc2 + term
    out2 = keep(acc2, g2_ref[...], b2_ref[...])
    coarse = dot(out2, pick2) + dot(up_ref[...], chosen3)
    lane = iota((body2, 2 * LANES), 1)
    image = iota((body2, 2 * LANES), 0) % PAIR
    flag = (lane >= LANES) & (lane % HALF == kept - HALF)
    coarse = jnp.where(flag, jnp.where(image < count, 1.0, 0.0), coarse)

    zero = jnp.zeros((HALF, HALF), jnp.bfloat16)
    for dy in range(3):
        taps = [w1_ref[dy, 0], w1_ref[dy, 1], w1_ref[dy, 2]]
        wgt1[dy, 0:HALF, :] = jnp.concatenate([taps[1], taps[0]], axis=1)
        wgt1[dy, HALF : 2 * HALF, :] = jnp.concatenate([taps[2], taps[1]], axis=1)
        wgt1[dy, 2 * HALF : 3 * HALF, :] = jnp.concatenate([zero, taps[2]], axis=1)
        wgt1[dy, 3 * HALF :, :] = jnp.concatenate([taps[0], zero], axis=1)
    body1 = h1 * rows2
    native1 = h1 * PAIR
    buf1[0:rows2, :] = jnp.zeros((rows2, buf1.shape[1]), jnp.bfloat16)
    buf1[rows2 + body1 :, :] = jnp.zeros((rows2, buf1.shape[1]), jnp.bfloat16)
    for first in range(0, h1, group):
        lines = min(group, h1 - first)
        block = s1_ref[first * native1 : (first + lines) * native1, :]
        twice = jnp.concatenate([block, block], axis=1)
        lower = iota((lines * rows2, LANES), 1) < HALF
        moved = [dot(p1_ref[t, : lines * rows2, : lines * native1], twice) for t in range(4)]
        start = (1 + first) * rows2
        stop = start + lines * rows2
        buf1[start:stop, 0:LANES] = jnp.where(lower, moved[0], moved[1]).astype(jnp.bfloat16)
        buf1[start:stop, LANES:] = jnp.where(lower, moved[2], moved[3]).astype(jnp.bfloat16)
    acc1 = None
    for dy in range(3):
        term = dot(buf1[dy * rows2 : dy * rows2 + body1, :], wgt1[dy])
        acc1 = term if acc1 is None else acc1 + term
    gain1 = jnp.concatenate([g1_ref[...], g1_ref[...]], axis=1)
    bias1 = jnp.concatenate([b1_ref[...], b1_ref[...]], axis=1)
    out1 = keep(acc1, gain1, bias1)
    fine = dot(out1, pick1)
    spread = jnp.broadcast_to(
        coarse[:, :LANES].reshape(h2, 1, rows2, LANES), (h2, PAIR, rows2, LANES)
    ).reshape(body1, LANES)
    fine = (fine + spread).astype(jnp.bfloat16)
    coarse = coarse[:, LANES:].astype(jnp.bfloat16)

    lines = h1 // owners
    lower = iota((PAIR * rows2, LANES), 1) < HALF
    for owner in range(owners):
        base = owner * lines // PAIR
        wide = fine[owner * lines * rows2 : (owner + 1) * lines * rows2, :]
        front = coarse[base * rows2 : (base + PAIR) * rows2, :]
        back = coarse[(base + PAIR) * rows2 : (base + 2 * PAIR) * rows2, :]
        narrow = jnp.where(lower, front, back)
        packed = dot(c1_ref[...], wide) + dot(c2_ref[...], narrow)
        out_ref[owner] = packed.astype(jnp.bfloat16)


def merge_kernel(p_ref, a_ref, b_ref, c_ref, d_ref, out_ref):
    piece = LANES // 4
    for part in range(out_ref.shape[0] // LANES):
        rows = slice(part * piece, (part + 1) * piece)
        stack = jnp.concatenate([r[rows, :] for r in (a_ref, b_ref, c_ref, d_ref)], axis=0)
        out_ref[part * LANES : (part + 1) * LANES, :] = dot(p_ref[...], stack).astype(jnp.bfloat16)


def covariance_kernel(dims, *refs):
    shards, lines, columns, kept, depth, pairs, steps = dims
    idx_ref = refs[0]
    shard_refs = refs[1 : 1 + shards]
    mean_ref, cov_ref = refs[1 + shards : 3 + shards]
    narrow, wide, table, eye, means, out, sems, *grams = refs[3 + shards :]
    images = narrow.shape[1]
    each = images // shards
    fine = lines * columns
    block = cov_ref.shape[0]
    size = pairs * PAIR

    for j in range(shards):
        at = slice(fine, fine + PAIR * columns)
        narrow[:, j * each : (j + 1) * each, :] = shard_refs[j][at]
    rank = rank_row(padded_index(idx_ref)).astype(jnp.int32)
    rank = jnp.concatenate([rank, rank], axis=1)
    r = iota((LANES, 2 * LANES), 0)
    c = iota((LANES, 2 * LANES), 1)
    table[0:LANES, :] = one_hot((rank == r % HALF) & (r // HALF == c // LANES))
    table[LANES:, :] = one_hot(rank - HALF == r % HALF)
    square = (depth, LANES)
    eye[...] = jnp.where(iota(square, 0) == iota(square, 1), 0.01, 0.0)

    def products(step, into):
        first = step * pairs
        odd = (lines * lax.axis_index("pos")) % PAIR
        lane = iota((images, LANES), 1)
        packs = [s[pl.ds(first, pairs)] for s in shard_refs]
        rows = []
        for t in range(pairs):
            level = ((first + t) // columns + odd) // PAIR
            left = jnp.concatenate([s[t] for s in packs], axis=0)
            right = narrow[(level % PAIR) * columns + (first + t) % columns]
            right = jnp.where(lane // HALF == level // PAIR, right, jnp.zeros_like(right))
            rows.append(jnp.concatenate([left, right], axis=1))
        values = dot(jnp.concatenate(rows, axis=0), table[...])
        wide[...] = values.astype(jnp.bfloat16)

        sums = jnp.sum(values.reshape(pairs, images, 2 * LANES), axis=1)
        total = sums[0:1, kept : kept + 1]
        mean = sums / total
        inverse = jnp.broadcast_to(1.0 / (total - 1.0), (1, LANES))
        a, b, c = pieces(sums)
        d, e, f = pieces(-mean)
        row = iota((16, 2 * LANES), 0)
        zero = jnp.zeros((images + 16, LANES), jnp.bfloat16)
        for t in range(pairs):
            at = slice(t, t + 1)
            third = jnp.where(row == 5, c[at], 0.0)
            left = jnp.where(row < 3, a[at], jnp.where(row < 5, b[at], third))
            third = jnp.where(row == 2, f[at], 0.0)
            right = jnp.where((row == 1) | (row == 4), e[at], third)
            right = jnp.where((row == 0) | (row == 3) | (row == 5), d[at], right)
            left, right = left.astype(jnp.bfloat16), right.astype(jnp.bfloat16)
            pair = wide[t * images : (t + 1) * images, :]
            even, other = pair[:, :LANES], pair[:, LANES:]
            stack = jnp.concatenate([even, left[:, :LANES], other, left[:, LANES:]], axis=0)
            even = jnp.concatenate([even, right[:, :LANES]], axis=0)
            other = jnp.concatenate([other, right[:, LANES:]], axis=0)
            block = jnp.concatenate(
                [
                    jnp.concatenate([even, zero], axis=1),
                    jnp.concatenate([zero, other], axis=1),
                ],
                axis=0,
            )
            moment = lax.dot_general(
                stack, block, (((0,), (0,)), ((), ())), preferred_element_type=jnp.float32
            )
            for side in range(PAIR):
                position = t * PAIR + side
                half = slice(side * LANES, (side + 1) * LANES)
                means[pl.ds(step * size + position, 1), :] = mean[at, half]
                start = (position % 8) * depth
                value = moment[:depth, half] * inverse + eye[...]
                into[position // 8][start : start + depth, :] = value

    def copy_out(step, count):
        rows = pl.ds(step * size if isinstance(step, int) else pl.multiple_of(step * size, size), count)
        return pltpu.make_async_copy(out.at[rows], cov_ref.at[rows], sems.at[step])

    def rows_out(step, source, count):
        for part, gram in enumerate(source):
            at = step * size + part * 8
            rows = pl.ds(at if isinstance(at, int) else pl.multiple_of(at, 8), 8)
            for k in range(kept):
                value = gram[pl.ds(k, 8, stride=depth), :]
                out[rows, k * kept : (k + 1) * kept] = value[:, :kept]
        copy_out(step, count).start()

    ready, coming = grams[: len(grams) // 2], grams[len(grams) // 2 :]
    tail = block - (steps - 1) * size
    products(0, ready)

    def two_steps(i, carry):
        products(2 * i + 1, coming)
        rows_out(2 * i, ready, size)
        products(2 * i + 2, ready)
        rows_out(2 * i + 1, coming, size)
        return carry

    lax.fori_loop(0, (steps - 1) // 2, two_steps, 0)
    if steps % 2 == 0:
        products(steps - 1, coming)
        rows_out(steps - 2, ready, size)
        ready = coming
    rows_out(steps - 1, ready, tail)
    mean_ref[...] = means[:block, :kept]
    for step in range(steps):
        copy_out(step, size if step < steps - 1 else tail).wait()


def shift_tables(h1, h2, h3, owners, group, pitch2, pitch3):
    rows2 = pitch2 * PAIR
    p1 = np.zeros((4, group * rows2, group * h1 * PAIR), np.float32)
    p2 = np.zeros((3, group * rows2, group * h2 * PAIR), np.float32)
    for y in range(group):
        for x in range(h2):
            for i in range(PAIR):
                to = y * rows2 + x * PAIR + i
                for t, source in enumerate((2 * x, 2 * x + 1, 2 * x + 2, 2 * x - 1)):
                    if 0 <= source < h1:
                        p1[t, to, (y * h1 + source) * PAIR + i] = 1
                for t in range(3):
                    if 0 <= x + t - 1 < h2:
                        p2[t, to, (y * h2 + x + t - 1) * PAIR + i] = 1
    p3 = np.zeros((3, h3 * pitch3 * PAIR, h3 * h3 * PAIR), np.float32)
    for y in range(h3):
        for x in range(h3):
            for i in range(PAIR):
                for t in range(3):
                    if 0 <= x + t - 1 < h3:
                        p3[t, (y * pitch3 + x) * PAIR + i, (y * h3 + x + t - 1) * PAIR + i] = 1
    up = np.zeros((h2 * rows2, h3 * pitch3 * PAIR), np.float32)
    for y in range(h2):
        for x in range(h2):
            for i in range(PAIR):
                up[y * rows2 + x * PAIR + i, ((y // 2) * pitch3 + x // 2) * PAIR + i] = 1
    lines = h1 // owners
    packed = pack_rows(h1, owners)
    c1 = np.zeros((packed, lines * rows2), np.float32)
    c2 = np.zeros((packed, PAIR * rows2), np.float32)
    for x in range(h2):
        for i in range(PAIR):
            for y in range(lines):
                c1[(y * h2 + x) * PAIR + i, y * rows2 + x * PAIR + i] = 1
            for y in range(PAIR):
                c2[((lines + y) * h2 + x) * PAIR + i, y * rows2 + x * PAIR + i] = 1
    return [jnp.asarray(a, jnp.bfloat16) for a in (p1, p2, p3, up, c1, c2)]


def pack_rows(h1, owners):
    lines = h1 // owners
    rows = (lines + PAIR) * (h1 // 2) * PAIR
    return -(-rows // 32) * 32


def merge_table():
    table = np.zeros((LANES, LANES), np.float32)
    for r in range(16):
        for s in range(4):
            for i in range(PAIR):
                table[r * 8 + s * PAIR + i, s * 32 + r * PAIR + i] = 1
    return jnp.asarray(table, jnp.bfloat16)


def whole(array):
    zeros = (0,) * array.ndim
    return pl.BlockSpec(array.shape, lambda g: zeros, pipeline_mode=pl.Buffered(1))


def packed_path(
    section_one,
    section_two,
    section_three,
    weight_one,
    weight_two,
    weight_three,
    gain_one,
    gain_two,
    gain_three,
    bias_one,
    bias_two,
    bias_three,
    channel_index,
    valid_count,
):
    slots, h1 = section_one.shape[:2]
    h2, h3 = section_two.shape[1], section_three.shape[1]
    c1, c2, c3 = section_one.shape[3], section_two.shape[3], section_three.shape[3]
    kept = channel_index.shape[0]
    owners = lax.axis_size("pos")
    groups = lax.axis_size("img")
    group, pitch2, pitch3 = 4, 16, 8
    tables = shift_tables(h1, h2, h3, owners, group, pitch2, pitch3)
    packed = pack_rows(h1, owners)
    rows2, rows3 = pitch2 * PAIR, pitch3 * PAIR

    def flat(section):
        return jnp.transpose(section, (1, 2, 0, 3)).reshape(-1, section.shape[3])

    index = channel_index.reshape(1, kept)
    smem = pl.BlockSpec(memory_space=pltpu.SMEM)
    operands = [
        flat(section_one),
        flat(section_two),
        flat(section_three),
        weight_one,
        weight_two,
        weight_three,
        gain_one.reshape(1, c1),
        gain_two.reshape(1, c2),
        gain_three.reshape(1, c3),
        bias_one.reshape(1, c1),
        bias_two.reshape(1, c2),
        bias_three.reshape(1, c3),
        index,
    ]
    packs_shape = jax.ShapeDtypeStruct((owners, packed, LANES), jnp.bfloat16)
    packs = pl.pallas_call(
        functools.partial(
            features_kernel, (h1, h2, h3, owners, kept, group, pitch2, pitch3)
        ),
        out_shape=packs_shape,
        grid=(1,),
        in_specs=[whole(a) for a in operands] + [smem] + [whole(a) for a in tables],
        out_specs=whole(packs_shape),
        scratch_shapes=[
            pltpu.VMEM(((h1 + 2) * rows2, 2 * LANES), jnp.bfloat16),
            pltpu.VMEM(((h2 + 2) * rows2, 3 * LANES), jnp.bfloat16),
            pltpu.VMEM(((h3 + 2) * rows3, 3 * c3), jnp.bfloat16),
            pltpu.VMEM((3, 2 * LANES, LANES), jnp.bfloat16),
        ],
        name="features",
    )(*operands, valid_count, *tables)

    me = lax.axis_index("pos")
    parts = [lax.dynamic_index_in_dim(packs, me, 0, keepdims=False)]
    for k in range(1, owners):
        pairs = [(i, i ^ k) for i in range(owners)]
        piece = lax.dynamic_index_in_dim(packs, me ^ k, 0, keepdims=False)
        parts.append(lax.ppermute(piece, "pos", pairs))
    merged_shape = jax.ShapeDtypeStruct((packed * owners, LANES), jnp.bfloat16)
    merging = [merge_table(), *parts]
    merged = pl.pallas_call(
        merge_kernel,
        out_shape=merged_shape,
        grid=(1,),
        in_specs=[whole(a) for a in merging],
        out_specs=whole(merged_shape),
        name="merge",
    )(*merging)

    levels = groups // PAIR
    shards = [merged]
    turns = sorted(range(1, levels), key=lambda t: (min(t, levels - t), t))
    for turn in turns:
        pairs = [
            (z * PAIR + c, ((z + turn) % levels) * PAIR + c)
            for z in range(levels)
            for c in range(PAIR)
        ]
        shards.append(lax.ppermute(merged, "img", pairs))
    swap = [(i, i ^ 1) for i in range(groups)]
    shards = shards + [lax.ppermute(s, "img", swap) for s in shards]

    lines, columns = h1 // owners, h2
    block = lines * h1
    each = owners * slots
    images = each * len(shards)
    shards = [s.reshape(packed // PAIR, each, LANES) for s in shards]
    parts = 2
    steps = -(-block // (8 * parts))
    depth = -(-(kept + 1) // 8) * 8
    pairs = 4 * parts
    size = 8 * parts
    mean_shape = jax.ShapeDtypeStruct((block, kept), jnp.float32)
    mean, covariance = pl.pallas_call(
        functools.partial(
            covariance_kernel, (len(shards), lines, columns, kept, depth, pairs, steps)
        ),
        out_shape=(mean_shape, jax.ShapeDtypeStruct((block, kept * kept), jnp.float32)),
        grid=(1,),
        in_specs=[whole(index)] + [whole(s) for s in shards],
        out_specs=(whole(mean_shape), pl.BlockSpec(memory_space=pl.ANY)),
        scratch_shapes=[
            pltpu.VMEM((PAIR * columns, images, LANES), jnp.bfloat16),
            pltpu.VMEM((pairs * images, 2 * LANES), jnp.bfloat16),
            pltpu.VMEM((2 * LANES, 2 * LANES), jnp.bfloat16),
            pltpu.VMEM((depth, LANES), jnp.float32),
            pltpu.VMEM((steps * size, LANES), jnp.float32),
            pltpu.VMEM((steps * size, kept * kept), jnp.float32),
            pltpu.SemaphoreType.DMA((steps,)),
        ]
        + [pltpu.VMEM((8 * depth, LANES), jnp.float32) for _ in range(2 * parts)],
        name="covariance",
    )(index, *shards)
    return mean.T, covariance


def suits(mesh, section_one, section_two, section_three, channel_index):
    owners, groups = mesh.shape["pos"], mesh.shape["img"]
    devices = owners * groups
    images, h1, _, c1 = section_one.shape
    h2, c2 = section_two.shape[1], section_two.shape[3]
    h3, c3 = section_three.shape[1], section_three.shape[3]
    kept = channel_index.shape[0]
    lines = h1 // owners
    return (
        images == PAIR * devices
        and owners == 4
        and groups % PAIR == 0
        and h1 % owners == 0
        and h1 == 2 * h2 == 4 * h3
        and h2 <= 16
        and h3 <= 8
        and (c1, c2, c3) == (HALF, LANES, 2 * LANES)
        and HALF <= kept < LANES
        and kept - HALF < HALF
        and lines == 7
    )


def solution(mesh):
    in_specs = (
        P(("img", "pos"), None, None, None),
        P(("img", "pos"), None, None, None),
        P(("img", "pos"), None, None, None),
        P(),
        P(),
        P(),
        P(),
        P(),
        P(),
        P(),
        P(),
        P(),
        P(),
        P("img", "pos"),
    )

    def run(*arrays):
        chosen = suits(mesh, arrays[0], arrays[1], arrays[2], arrays[12])
        return jax.shard_map(
            packed_path if chosen else plain,
            mesh=mesh,
            in_specs=in_specs,
            out_specs=(P(None, "pos"), P("pos", None)),
            check_vma=False,
        )(*arrays)

    return run
```

```python
import functools

import jax
import jax.numpy as jnp
import numpy as np
from jax import lax
from jax.experimental import pallas as pl
from jax.experimental.pallas import tpu as pltpu
from jax.sharding import PartitionSpec as P

LANES = 128
HALF = 64
PAIR = 2


def section_out(images, weight, gain, bias):
    conv = lax.conv_general_dilated(
        images,
        weight,
        (1, 1),
        "SAME",
        dimension_numbers=("NHWC", "HWIO", "NHWC"),
        preferred_element_type=jnp.float32,
    )
    return jax.nn.relu(conv * gain + bias).astype(jnp.bfloat16)


def pick_channels(section, offset, width, channel_index):
    table = (channel_index[None, :] - offset == lax.iota(jnp.int32, width)[:, None]).astype(
        jnp.bfloat16
    )
    return jnp.einsum("ihwc,ck->ikhw", section, table, preferred_element_type=jnp.float32).astype(
        jnp.bfloat16
    )


def widen(picked, factor):
    return jnp.repeat(jnp.repeat(picked, factor, axis=2), factor, axis=3)


def pair_outer(rows):
    return (rows[:, :, None] * rows[:, None, :]).reshape(
        rows.shape[0], rows.shape[1] * rows.shape[1]
    )


def product_rows(values):
    kept = values.shape[1]
    raw = jnp.einsum("ikp,ilp->pkl", values, values, preferred_element_type=jnp.float32)
    return raw.reshape(values.shape[2], kept * kept)


def plain(
    section_one,
    section_two,
    section_three,
    weight_one,
    weight_two,
    weight_three,
    gain_one,
    gain_two,
    gain_three,
    bias_one,
    bias_two,
    bias_three,
    channel_index,
    valid_count,
):
    slots = section_one.shape[0]
    side = section_one.shape[1]
    width_one = section_one.shape[3]
    width_two = section_two.shape[3]
    width_three = section_three.shape[3]
    kept = channel_index.shape[0]
    owners = lax.axis_size("pos")
    block = side * side // owners
    own_count = valid_count[0, 0]
    scale = (lax.iota(jnp.int32, slots) < own_count).astype(jnp.bfloat16)[:, None, None, None]
    out_one = section_out(section_one, weight_one, gain_one, bias_one) * scale
    out_two = section_out(section_two, weight_two, gain_two, bias_two) * scale
    out_three = section_out(section_three, weight_three, gain_three, bias_three) * scale
    features = pick_channels(out_one, 0, width_one, channel_index)
    features = features + widen(pick_channels(out_two, width_one, width_two, channel_index), 2)
    features = features + widen(
        pick_channels(out_three, width_one + width_two, width_three, channel_index), 4
    )
    shaped = features.reshape(slots, kept, owners, block)
    group = lax.psum(own_count, "pos").astype(jnp.float32)
    owned = lax.all_to_all(shaped, "pos", split_axis=2, concat_axis=0, tiled=True)[:, :, 0, :]
    values = lax.all_gather(owned, "img", axis=0, tiled=True)
    counts = lax.all_gather(group.astype(jnp.bfloat16)[None], "img", axis=0, tiled=True)
    total = jnp.sum(counts.astype(jnp.float32))
    all_sums = jnp.sum(values, axis=0, dtype=jnp.float32).T
    all_raw = product_rows(values)
    mean = all_sums / total
    moment = all_raw - total * pair_outer(mean)
    covariance = moment / (total - 1.0) + 0.01 * jnp.eye(kept, dtype=jnp.float32).reshape(
        1, kept * kept
    )
    return (mean.T, covariance)


def dot(a, b):
    return lax.dot_general(a, b, (((1,), (0,)), ((), ())), preferred_element_type=jnp.float32)


def iota(shape, dim):
    return lax.broadcasted_iota(jnp.int32, shape, dim)


def padded_index(idx_ref):
    kept = idx_ref.shape[1]
    lane = iota((1, LANES), 1)
    row = jnp.concatenate([idx_ref[...], jnp.zeros((1, LANES - kept), jnp.int32)], axis=1)
    return jnp.where(lane < kept, row, 100000 + lane).astype(jnp.float32)


def column_of(row):
    spread = jnp.broadcast_to(row, (LANES, LANES))
    diagonal = iota((LANES, LANES), 0) == iota((LANES, LANES), 1)
    return jnp.sum(jnp.where(diagonal, spread, 0.0), axis=1, keepdims=True)


def rank_row(idx_row):
    smaller = column_of(idx_row) < idx_row
    return jnp.sum(jnp.where(smaller, 1.0, 0.0), axis=0, keepdims=True)


def one_hot(mask):
    return jnp.where(mask, 1.0, 0.0).astype(jnp.bfloat16)


def pieces(values):
    found = []
    for _ in range(3):
        piece = values.astype(jnp.bfloat16).astype(jnp.float32)
        found.append(piece)
        values = values - piece
    return found


def neighbours(rows):
    count = rows.shape[0]
    return pltpu.roll(rows, PAIR, 0), rows, pltpu.roll(rows, count - PAIR, 0)


def features_kernel(dims, *refs):
    names = "s1 p1 w1 g1 b1 index s2 p2 w2 g2 b2 s3 p3 w3 g3 b3 up c1 c2".split()
    given, outs, scratch = refs[: len(names) + 1], refs[len(names) + 1 :][: dims[3]], refs[len(names) + 1 + dims[3] :]
    count_ref = given[-1]
    buf1, buf2, buf3, near3, wgt1, fines, coarses, sems = scratch[:8]
    held = dict(zip(names, scratch[8:]))
    copies = {}
    for n, name in enumerate(names):
        copies[name] = pltpu.make_async_copy(given[n], held[name], sems.at[n])
        copies[name].start()

    def get(name):
        if name in copies:
            copies.pop(name).wait()
        return held[name]

    h1, h2, h3, owners, kept, group, pitch2, pitch3 = dims
    count = count_ref[0, 0]
    base2, base3 = HALF, HALF + LANES

    def keep(values, gain, bias):
        image = iota((values.shape[0], 1), 0) % PAIR
        shaped = jnp.maximum(values * gain + bias, 0.0)
        return jnp.where(image < count, shaped, 0.0).astype(jnp.bfloat16)

    rows2 = pitch2 * PAIR
    zero = jnp.zeros((HALF, HALF), jnp.bfloat16)
    for dy in range(3):
        taps = [get("w1")[dy, 0], get("w1")[dy, 1], get("w1")[dy, 2]]
        wgt1[dy, 0:HALF, :] = jnp.concatenate([taps[1], taps[0]], axis=1)
        wgt1[dy, HALF : 2 * HALF, :] = jnp.concatenate([taps[2], taps[1]], axis=1)
        wgt1[dy, 2 * HALF : 3 * HALF, :] = jnp.concatenate([zero, taps[2]], axis=1)
        wgt1[dy, 3 * HALF :, :] = jnp.concatenate([taps[0], zero], axis=1)
    body1 = h1 * rows2
    native1 = h1 * PAIR
    buf1[0:rows2, :] = jnp.zeros((rows2, buf1.shape[1]), jnp.bfloat16)
    buf1[rows2 + body1 :, :] = jnp.zeros((rows2, buf1.shape[1]), jnp.bfloat16)
    for first in range(0, h1, group):
        lines = min(group, h1 - first)
        block = get("s1")[first * native1 : (first + lines) * native1, :]
        twice = jnp.concatenate([block, block], axis=1)
        lower = iota((lines * rows2, LANES), 1) < HALF
        moved = [dot(get("p1")[t, : lines * rows2, : lines * native1], twice) for t in range(PAIR)]
        start = (1 + first) * rows2
        stop = start + lines * rows2
        before, centre, after = neighbours(jnp.where(lower, moved[0], moved[1]))
        buf1[start:stop, 0:LANES] = centre.astype(jnp.bfloat16)
        buf1[start:stop, LANES:] = jnp.where(lower, after, before).astype(jnp.bfloat16)
    acc1 = None
    for dy in range(3):
        term = dot(buf1[dy * rows2 : dy * rows2 + body1, :], wgt1[dy])
        acc1 = term if acc1 is None else acc1 + term
    gain1 = jnp.concatenate([get("g1")[...], get("g1")[...]], axis=1)
    bias1 = jnp.concatenate([get("b1")[...], get("b1")[...]], axis=1)
    out1 = keep(acc1, gain1, bias1)
    index_row = padded_index(get("index"))
    rank_col = column_of(rank_row(index_row))
    slot = iota((LANES, LANES), 1).astype(jnp.float32)
    ranked = jnp.sum(jnp.where(rank_col == slot, column_of(index_row), 0.0), axis=0, keepdims=True)
    ranked = ranked.astype(jnp.int32)
    low = jnp.concatenate([ranked[:, :HALF], ranked[:, :HALF]], axis=1)
    high = jnp.concatenate([ranked[:, HALF:], ranked[:, HALF:]], axis=1)
    both = jnp.concatenate([low, high], axis=1)
    row128, lane128 = iota((LANES, LANES), 0), iota((LANES, LANES), 1)
    same_half = (row128 // HALF) == (lane128 // HALF)
    pick1 = one_hot((low == row128 % HALF) & same_half)
    pick2 = one_hot(both == base2 + iota((LANES, 2 * LANES), 0))
    pick3 = one_hot(both == base3 + iota((2 * LANES, 2 * LANES), 0))

    body2 = h2 * rows2
    native2 = h2 * PAIR
    buf2[0:rows2, :] = jnp.zeros((rows2, buf2.shape[1]), jnp.bfloat16)
    buf2[rows2 + body2 :, :] = jnp.zeros((rows2, buf2.shape[1]), jnp.bfloat16)
    for first in range(0, h2, group):
        lines = min(group, h2 - first)
        block = get("s2")[first * native2 : (first + lines) * native2, :]
        centre = dot(get("p2")[: lines * rows2, : lines * native2], block)
        start = (1 + first) * rows2
        for tap, moved in enumerate(neighbours(centre)):
            lanes = slice(tap * LANES, (tap + 1) * LANES)
            buf2[start : start + lines * rows2, lanes] = moved.astype(jnp.bfloat16)
    acc2 = None
    for dy in range(3):
        left = buf2[dy * rows2 : dy * rows2 + body2, :]
        term = dot(left, get("w2")[dy].reshape(3 * LANES, LANES))
        acc2 = term if acc2 is None else acc2 + term
    out2 = keep(acc2, get("g2")[...], get("b2")[...])
    rows3 = pitch3 * PAIR
    body3 = h3 * rows3
    buf3[0:rows3, :] = jnp.zeros((rows3, buf3.shape[1]), jnp.bfloat16)
    buf3[rows3 + body3 :, :] = jnp.zeros((rows3, buf3.shape[1]), jnp.bfloat16)
    for y in range(h3):
        for x in range(h3):
            at = (y * h3 + x) * PAIR
            near3[at : at + PAIR, :] = get("s3")[y, x]
    third = near3[...]
    width3 = buf3.shape[1] // 3
    centre = dot(get("p3")[:, : third.shape[0]], third)
    for tap, moved in enumerate(neighbours(centre)):
        lanes = slice(tap * width3, (tap + 1) * width3)
        buf3[rows3 : rows3 + body3, lanes] = moved.astype(jnp.bfloat16)
    acc3 = None
    for dy in range(3):
        for tap in range(3):
            left = buf3[dy * rows3 : dy * rows3 + body3, tap * width3 : (tap + 1) * width3]
            term = dot(left, get("w3")[dy, tap])
            acc3 = term if acc3 is None else acc3 + term
    out3 = keep(acc3, get("g3")[...], get("b3")[...])
    chosen3 = dot(out3, pick3).astype(jnp.bfloat16)

    coarse = dot(out2, pick2) + dot(get("up")[:, : h3 * pitch3 * PAIR], chosen3)
    lane = iota((body2, 2 * LANES), 1)
    image = iota((body2, 2 * LANES), 0) % PAIR
    flag = (lane >= LANES) & (lane % HALF == kept - HALF)
    coarse = jnp.where(flag, jnp.where(image < count, 1.0, 0.0), coarse)

    fine = dot(out1, pick1)
    spread = jnp.broadcast_to(
        coarse[:, :LANES].reshape(h2, 1, rows2, LANES), (h2, PAIR, rows2, LANES)
    ).reshape(body1, LANES)
    fine = (fine + spread).astype(jnp.bfloat16)
    coarse = coarse[:, LANES:].astype(jnp.bfloat16)

    fines[...] = fine
    coarses[...] = coarse
    lines = h1 // owners
    lower = iota((PAIR * rows2, LANES), 1) < HALF
    for k in range(owners):
        owner = lax.axis_index("pos") ^ k
        base = owner * lines // PAIR
        at = pl.multiple_of(owner * (lines * rows2), rows2)
        wide = fines[pl.ds(at, lines * rows2), :]
        front = coarses[pl.ds(pl.multiple_of(base * rows2, rows2), PAIR * rows2), :]
        back = coarses[pl.ds(pl.multiple_of((base + PAIR) * rows2, rows2), PAIR * rows2), :]
        narrow = jnp.where(lower, front, back)
        packed = dot(get("c1")[:, : lines * rows2], wide)
        packed = packed + dot(get("c2")[:, : PAIR * rows2], narrow)
        outs[k][...] = packed.astype(jnp.bfloat16)


def merge_kernel(*refs):
    *parts, out_ref = refs
    piece = LANES // len(parts)
    to, source = iota((LANES, LANES), 0), iota((LANES, LANES), 1)
    each = len(parts) * PAIR
    wanted = (to % each) // PAIR * piece + (to // each) * PAIR + to % PAIR
    table = one_hot(source == wanted)
    for block in range(out_ref.shape[0] // LANES):
        rows = slice(block * piece, (block + 1) * piece)
        stack = jnp.concatenate([part[rows, :] for part in parts], axis=0)
        out_ref[block * LANES : (block + 1) * LANES, :] = dot(table, stack).astype(jnp.bfloat16)


def covariance_kernel(dims, *refs):
    shards, lines, columns, kept, depth, pairs, steps = dims
    idx_ref = refs[0]
    shard_refs = refs[1 : 1 + shards]
    mean_ref, cov_ref = refs[1 + shards : 3 + shards]
    narrow, wide, table, eye, means, out, sems, *grams = refs[3 + shards :]
    images = narrow.shape[1]
    each = images // shards
    fine = lines * columns
    block = cov_ref.shape[0]
    size = pairs * PAIR

    for j in range(shards):
        at = slice(fine, fine + PAIR * columns)
        narrow[:, j * each : (j + 1) * each, :] = shard_refs[j][at]
    rank = rank_row(padded_index(idx_ref)).astype(jnp.int32)
    rank = jnp.concatenate([rank, rank], axis=1)
    r = iota((LANES, 2 * LANES), 0)
    c = iota((LANES, 2 * LANES), 1)
    table[0:LANES, :] = one_hot((rank == r % HALF) & (r // HALF == c // LANES))
    table[LANES:, :] = one_hot(rank - HALF == r % HALF)
    square = (depth, LANES)
    eye[...] = jnp.where(iota(square, 0) == iota(square, 1), 0.01, 0.0)

    def products(step, into):
        first = step * pairs
        odd = (lines * lax.axis_index("pos")) % PAIR
        lane = iota((images, LANES), 1)
        packs = [s[pl.ds(first, pairs)] for s in shard_refs]
        rows = []
        for t in range(pairs):
            level = ((first + t) // columns + odd) // PAIR
            left = jnp.concatenate([s[t] for s in packs], axis=0)
            right = narrow[(level % PAIR) * columns + (first + t) % columns]
            right = jnp.where(lane // HALF == level // PAIR, right, jnp.zeros_like(right))
            rows.append(jnp.concatenate([left, right], axis=1))
        values = dot(jnp.concatenate(rows, axis=0), table[...])
        wide[...] = values.astype(jnp.bfloat16)

        sums = jnp.sum(values.reshape(pairs, images, 2 * LANES), axis=1)
        total = sums[0:1, kept : kept + 1]
        mean = sums / total
        inverse = jnp.broadcast_to(1.0 / (total - 1.0), (1, LANES))
        a, b, c = pieces(sums)
        d, e, f = pieces(-mean)
        row = iota((16, 2 * LANES), 0)
        zero = jnp.zeros((images + 16, LANES), jnp.bfloat16)
        for t in range(pairs):
            at = slice(t, t + 1)
            third = jnp.where(row == 5, c[at], 0.0)
            left = jnp.where(row < 3, a[at], jnp.where(row < 5, b[at], third))
            third = jnp.where(row == 2, f[at], 0.0)
            right = jnp.where((row == 1) | (row == 4), e[at], third)
            right = jnp.where((row == 0) | (row == 3) | (row == 5), d[at], right)
            left, right = left.astype(jnp.bfloat16), right.astype(jnp.bfloat16)
            pair = wide[t * images : (t + 1) * images, :]
            even, other = pair[:, :LANES], pair[:, LANES:]
            stack = jnp.concatenate([even, left[:, :LANES], other, left[:, LANES:]], axis=0)
            even = jnp.concatenate([even, right[:, :LANES]], axis=0)
            other = jnp.concatenate([other, right[:, LANES:]], axis=0)
            block = jnp.concatenate(
                [
                    jnp.concatenate([even, zero], axis=1),
                    jnp.concatenate([zero, other], axis=1),
                ],
                axis=0,
            )
            moment = lax.dot_general(
                stack, block, (((0,), (0,)), ((), ())), preferred_element_type=jnp.float32
            )
            for side in range(PAIR):
                position = t * PAIR + side
                half = slice(side * LANES, (side + 1) * LANES)
                means[pl.ds(step * size + position, 1), :] = mean[at, half]
                start = (position % 8) * depth
                value = moment[:depth, half] * inverse + eye[...]
                into[position // 8][start : start + depth, :] = value

    def copy_out(step, count):
        rows = pl.ds(step * size if isinstance(step, int) else pl.multiple_of(step * size, size), count)
        return pltpu.make_async_copy(out.at[rows], cov_ref.at[rows], sems.at[step])

    def rows_out(step, source, count):
        for part, gram in enumerate(source):
            at = step * size + part * 8
            rows = pl.ds(at if isinstance(at, int) else pl.multiple_of(at, 8), 8)
            for k in range(kept):
                value = gram[pl.ds(k, 8, stride=depth), :]
                out[rows, k * kept : (k + 1) * kept] = value[:, :kept]
        copy_out(step, count).start()

    ready, coming = grams[: len(grams) // 2], grams[len(grams) // 2 :]
    tail = block - (steps - 1) * size
    products(0, ready)

    def two_steps(i, carry):
        products(2 * i + 1, coming)
        rows_out(2 * i, ready, size)
        products(2 * i + 2, ready)
        rows_out(2 * i + 1, coming, size)
        return carry

    lax.fori_loop(0, (steps - 1) // 2, two_steps, 0)
    if steps % 2 == 0:
        products(steps - 1, coming)
        rows_out(steps - 2, ready, size)
        ready = coming
    rows_out(steps - 1, ready, tail)
    mean_ref[...] = means[:block, :kept]
    for step in range(steps):
        copy_out(step, size if step < steps - 1 else tail).wait()


def shift_tables(h1, h2, h3, owners, group, pitch2, pitch3):
    rows2 = pitch2 * PAIR
    p1 = np.zeros((PAIR, group * rows2, group * h1 * PAIR), np.float32)
    p2 = np.zeros((group * rows2, group * h2 * PAIR), np.float32)
    for y in range(group):
        for x in range(h2):
            for i in range(PAIR):
                to = y * rows2 + x * PAIR + i
                for t in range(PAIR):
                    p1[t, to, (y * h1 + 2 * x + t) * PAIR + i] = 1
                p2[to, (y * h2 + x) * PAIR + i] = 1
    p3 = np.zeros((h3 * pitch3 * PAIR, h3 * h3 * PAIR), np.float32)
    for y in range(h3):
        for x in range(h3):
            for i in range(PAIR):
                p3[(y * pitch3 + x) * PAIR + i, (y * h3 + x) * PAIR + i] = 1
    up = np.zeros((h2 * rows2, h3 * pitch3 * PAIR), np.float32)
    for y in range(h2):
        for x in range(h2):
            for i in range(PAIR):
                up[y * rows2 + x * PAIR + i, ((y // 2) * pitch3 + x // 2) * PAIR + i] = 1
    lines = h1 // owners
    packed = pack_rows(h1, owners)
    c1 = np.zeros((packed, lines * rows2), np.float32)
    c2 = np.zeros((packed, PAIR * rows2), np.float32)
    for x in range(h2):
        for i in range(PAIR):
            for y in range(lines):
                c1[(y * h2 + x) * PAIR + i, y * rows2 + x * PAIR + i] = 1
            for y in range(PAIR):
                c2[((lines + y) * h2 + x) * PAIR + i, y * rows2 + x * PAIR + i] = 1
    tables = []
    for a in (p1, p2, p3, up, c1, c2):
        room = [(0, 0)] * (a.ndim - 1) + [(0, -a.shape[-1] % LANES)]
        tables.append(jnp.asarray(np.pad(a, room), jnp.bfloat16))
    return tables


def pack_rows(h1, owners):
    lines = h1 // owners
    rows = (lines + PAIR) * (h1 // 2) * PAIR
    return -(-rows // 32) * 32


def packed_path(
    section_one,
    section_two,
    section_three,
    weight_one,
    weight_two,
    weight_three,
    gain_one,
    gain_two,
    gain_three,
    bias_one,
    bias_two,
    bias_three,
    channel_index,
    valid_count,
):
    slots, h1 = section_one.shape[:2]
    h2, h3 = section_two.shape[1], section_three.shape[1]
    c1, c2, c3 = section_one.shape[3], section_two.shape[3], section_three.shape[3]
    kept = channel_index.shape[0]
    owners = lax.axis_size("pos")
    groups = lax.axis_size("img")
    group, pitch2, pitch3 = 4, 16, 8
    tables = shift_tables(h1, h2, h3, owners, group, pitch2, pitch3)
    packed = pack_rows(h1, owners)
    rows2, rows3 = pitch2 * PAIR, pitch3 * PAIR

    def flat(section):
        return jnp.transpose(section, (1, 2, 0, 3)).reshape(-1, section.shape[3])

    index = channel_index.reshape(1, kept)
    smem = pl.BlockSpec(memory_space=pltpu.SMEM)
    vmem = pl.BlockSpec(memory_space=pltpu.VMEM)
    third = jnp.transpose(section_three, (1, 2, 0, 3))
    p1, p2, p3, up, pack1, pack2 = tables
    operands = [
        *(flat(section_one), p1, weight_one, gain_one.reshape(1, c1), bias_one.reshape(1, c1)),
        index,
        *(flat(section_two), p2, weight_two, gain_two.reshape(1, c2), bias_two.reshape(1, c2)),
        *(third, p3, weight_three, gain_three.reshape(1, c3), bias_three.reshape(1, c3)),
        *(up, pack1, pack2),
    ]
    packs_shape = jax.ShapeDtypeStruct((packed, LANES), jnp.bfloat16)
    packs = pl.pallas_call(
        functools.partial(features_kernel, (h1, h2, h3, owners, kept, group, pitch2, pitch3)),
        out_shape=[packs_shape] * owners,
        in_specs=[pl.BlockSpec(memory_space=pl.ANY)] * len(operands) + [smem],
        out_specs=[pl.BlockSpec((packed, LANES), lambda: (0, 0))] * owners,
        scratch_shapes=[
            pltpu.VMEM(((h1 + 2) * rows2, 2 * LANES), jnp.bfloat16),
            pltpu.VMEM(((h2 + 2) * rows2, 3 * LANES), jnp.bfloat16),
            pltpu.VMEM(((h3 + 2) * rows3, 3 * c3), jnp.bfloat16),
            pltpu.VMEM((h3 * h3 * PAIR, c3), jnp.bfloat16),
            pltpu.VMEM((3, 2 * LANES, LANES), jnp.bfloat16),
            pltpu.VMEM((h1 * rows2, LANES), jnp.bfloat16),
            pltpu.VMEM((h2 * rows2, LANES), jnp.bfloat16),
            pltpu.SemaphoreType.DMA((len(operands),)),
        ]
        + [pltpu.VMEM(a.shape, a.dtype) for a in operands],
        name="features",
    )(*operands, valid_count)

    parts = [packs[0]]
    for k in range(1, owners):
        pairs = [(i, i ^ k) for i in range(owners)]
        parts.append(lax.ppermute(packs[k], "pos", pairs))
    merged_shape = jax.ShapeDtypeStruct((packed * owners, LANES), jnp.bfloat16)
    merged = pl.pallas_call(
        merge_kernel,
        out_shape=merged_shape,
        in_specs=[vmem] * owners,
        out_specs=vmem,
        compiler_params=pltpu.CompilerParams(vmem_limit_bytes=8 << 20),
        name="merge",
    )(*parts)

    levels = groups // PAIR
    shards = [merged]
    turns = sorted(range(1, levels), key=lambda t: (min(t, levels - t), t))
    for turn in turns:
        pairs = [
            (z * PAIR + c, ((z + turn) % levels) * PAIR + c)
            for z in range(levels)
            for c in range(PAIR)
        ]
        shards.append(lax.ppermute(merged, "img", pairs))
    swap = [(i, i ^ 1) for i in range(groups)]
    shards = shards + [lax.ppermute(s, "img", swap) for s in shards]

    lines, columns = h1 // owners, h2
    block = lines * h1
    each = owners * slots
    images = each * len(shards)
    shards = [s.reshape(packed // PAIR, each, LANES) for s in shards]
    parts = 2
    steps = -(-block // (8 * parts))
    depth = -(-(kept + 1) // 8) * 8
    pairs = 4 * parts
    size = 8 * parts
    mean_shape = jax.ShapeDtypeStruct((block, kept), jnp.float32)
    mean, covariance = pl.pallas_call(
        functools.partial(
            covariance_kernel, (len(shards), lines, columns, kept, depth, pairs, steps)
        ),
        out_shape=(mean_shape, jax.ShapeDtypeStruct((block, kept * kept), jnp.float32)),
        in_specs=[vmem] * (1 + len(shards)),
        out_specs=(vmem, pl.BlockSpec(memory_space=pl.ANY)),
        compiler_params=pltpu.CompilerParams(vmem_limit_bytes=24 << 20),
        scratch_shapes=[
            pltpu.VMEM((PAIR * columns, images, LANES), jnp.bfloat16),
            pltpu.VMEM((pairs * images, 2 * LANES), jnp.bfloat16),
            pltpu.VMEM((2 * LANES, 2 * LANES), jnp.bfloat16),
            pltpu.VMEM((depth, LANES), jnp.float32),
            pltpu.VMEM((steps * size, LANES), jnp.float32),
            pltpu.VMEM((steps * size, kept * kept), jnp.float32),
            pltpu.SemaphoreType.DMA((steps,)),
        ]
        + [pltpu.VMEM((8 * depth, LANES), jnp.float32) for _ in range(2 * parts)],
        name="covariance",
    )(index, *shards)
    return mean.T, covariance


def suits(mesh, section_one, section_two, section_three, channel_index):
    owners, groups = mesh.shape["pos"], mesh.shape["img"]
    devices = owners * groups
    images, h1, _, c1 = section_one.shape
    h2, c2 = section_two.shape[1], section_two.shape[3]
    h3, c3 = section_three.shape[1], section_three.shape[3]
    kept = channel_index.shape[0]
    lines = h1 // owners
    return (
        images == PAIR * devices
        and owners == 4
        and groups % PAIR == 0
        and h1 % owners == 0
        and h1 == 2 * h2 == 4 * h3
        and h2 <= 16
        and h3 <= 8
        and (c1, c2, c3) == (HALF, LANES, 2 * LANES)
        and HALF <= kept < LANES
        and kept - HALF < HALF
        and lines == 7
    )


def solution(mesh):
    in_specs = (
        P(("img", "pos"), None, None, None),
        P(("img", "pos"), None, None, None),
        P(("img", "pos"), None, None, None),
        P(),
        P(),
        P(),
        P(),
        P(),
        P(),
        P(),
        P(),
        P(),
        P(),
        P("img", "pos"),
    )

    def run(*arrays):
        chosen = suits(mesh, arrays[0], arrays[1], arrays[2], arrays[12])
        return jax.shard_map(
            packed_path if chosen else plain,
            mesh=mesh,
            in_specs=in_specs,
            out_specs=(P(None, "pos"), P("pos", None)),
            check_vma=False,
        )(*arrays)

    return run
```

```python
import functools

import jax
import jax.numpy as jnp
import numpy as np
from jax import lax
from jax.experimental import pallas as pl
from jax.experimental.pallas import tpu as pltpu
from jax.sharding import PartitionSpec as P

LANES = 128
HALF = 64
THIRD = 42
QUARTER = 32
PAIR = 2


def section_out(images, weight, gain, bias):
    conv = lax.conv_general_dilated(
        images,
        weight,
        (1, 1),
        "SAME",
        dimension_numbers=("NHWC", "HWIO", "NHWC"),
        preferred_element_type=jnp.float32,
    )
    return jax.nn.relu(conv * gain + bias).astype(jnp.bfloat16)


def pick_channels(section, offset, width, channel_index):
    table = (channel_index[None, :] - offset == lax.iota(jnp.int32, width)[:, None]).astype(
        jnp.bfloat16
    )
    return jnp.einsum("ihwc,ck->ikhw", section, table, preferred_element_type=jnp.float32).astype(
        jnp.bfloat16
    )


def widen(picked, factor):
    return jnp.repeat(jnp.repeat(picked, factor, axis=2), factor, axis=3)


def pair_outer(rows):
    return (rows[:, :, None] * rows[:, None, :]).reshape(
        rows.shape[0], rows.shape[1] * rows.shape[1]
    )


def product_rows(values):
    kept = values.shape[1]
    raw = jnp.einsum("ikp,ilp->pkl", values, values, preferred_element_type=jnp.float32)
    return raw.reshape(values.shape[2], kept * kept)


def plain(
    section_one,
    section_two,
    section_three,
    weight_one,
    weight_two,
    weight_three,
    gain_one,
    gain_two,
    gain_three,
    bias_one,
    bias_two,
    bias_three,
    channel_index,
    valid_count,
):
    slots = section_one.shape[0]
    side = section_one.shape[1]
    width_one = section_one.shape[3]
    width_two = section_two.shape[3]
    width_three = section_three.shape[3]
    kept = channel_index.shape[0]
    owners = lax.axis_size("pos")
    block = side * side // owners
    own_count = valid_count[0, 0]
    scale = (lax.iota(jnp.int32, slots) < own_count).astype(jnp.bfloat16)[:, None, None, None]
    out_one = section_out(section_one, weight_one, gain_one, bias_one) * scale
    out_two = section_out(section_two, weight_two, gain_two, bias_two) * scale
    out_three = section_out(section_three, weight_three, gain_three, bias_three) * scale
    features = pick_channels(out_one, 0, width_one, channel_index)
    features = features + widen(pick_channels(out_two, width_one, width_two, channel_index), 2)
    features = features + widen(
        pick_channels(out_three, width_one + width_two, width_three, channel_index), 4
    )
    shaped = features.reshape(slots, kept, owners, block)
    group = lax.psum(own_count, "pos").astype(jnp.float32)
    owned = lax.all_to_all(shaped, "pos", split_axis=2, concat_axis=0, tiled=True)[:, :, 0, :]
    values = lax.all_gather(owned, "img", axis=0, tiled=True)
    counts = lax.all_gather(group.astype(jnp.bfloat16)[None], "img", axis=0, tiled=True)
    total = jnp.sum(counts.astype(jnp.float32))
    all_sums = jnp.sum(values, axis=0, dtype=jnp.float32).T
    all_raw = product_rows(values)
    mean = all_sums / total
    moment = all_raw - total * pair_outer(mean)
    covariance = moment / (total - 1.0) + 0.01 * jnp.eye(kept, dtype=jnp.float32).reshape(
        1, kept * kept
    )
    return (mean.T, covariance)


def dot(a, b):
    return lax.dot_general(a, b, (((1,), (0,)), ((), ())), preferred_element_type=jnp.float32)


def iota(shape, dim):
    return lax.broadcasted_iota(jnp.int32, shape, dim)


def padded_index(idx_ref):
    kept = idx_ref.shape[1]
    lane = iota((1, LANES), 1)
    row = jnp.concatenate([idx_ref[...], jnp.zeros((1, LANES - kept), jnp.int32)], axis=1)
    return jnp.where(lane < kept, row, 100000 + lane).astype(jnp.float32)


def column_of(row):
    spread = jnp.broadcast_to(row, (LANES, LANES))
    diagonal = iota((LANES, LANES), 0) == iota((LANES, LANES), 1)
    return jnp.sum(jnp.where(diagonal, spread, 0.0), axis=1, keepdims=True)


def rank_row(idx_row):
    smaller = column_of(idx_row) < idx_row
    return jnp.sum(jnp.where(smaller, 1.0, 0.0), axis=0, keepdims=True)


def one_hot(mask):
    return jnp.where(mask, 1.0, 0.0).astype(jnp.bfloat16)


def pieces(values):
    found = []
    for _ in range(3):
        piece = values.astype(jnp.bfloat16).astype(jnp.float32)
        found.append(piece)
        values = values - piece
    return found


def neighbours(rows):
    count = rows.shape[0]
    return pltpu.roll(rows, PAIR, 0), rows, pltpu.roll(rows, count - PAIR, 0)


def features_kernel(dims, *refs):
    names = "s1 p1 w1 g1 b1 index s2 p2 w2 g2 b2 s3 p3 w3 g3 b3 up c1 c2 k1 k2 k3".split()
    given = refs[: len(names) + 1]
    count_ref = given[-1]
    tops, rests, small_ref = refs[len(given) :][: dims[3]], refs[len(given) + dims[3] :][: dims[3]], refs[len(given) + 2 * dims[3]]
    scratch = refs[len(given) + 2 * dims[3] + 1 :]
    buf1, buf2, buf3, near3, wgt1, kept1, kept2, kept3, fines, coarses, thirds, sems = scratch[:12]
    held = dict(zip(names, scratch[12:]))
    copies = {}
    for n, name in enumerate(names):
        copies[name] = pltpu.make_async_copy(given[n], held[name], sems.at[n])
        copies[name].start()

    def get(name):
        if name in copies:
            copies.pop(name).wait()
        return held[name]

    h1, h2, h3, owners, kept, group, pitch2, pitch3 = dims
    count = count_ref[0, 0]
    base2, base3 = HALF, HALF + LANES

    def keep(values, gain, bias):
        image = iota((values.shape[0], 1), 0) % PAIR
        shaped = jnp.maximum(values * gain + bias, 0.0)
        return jnp.where(image < count, shaped, 0.0).astype(jnp.bfloat16)

    rows2 = pitch2 * PAIR
    zero = jnp.zeros((HALF, HALF), jnp.bfloat16)
    for dy in range(3):
        taps = [get("w1")[dy, 0], get("w1")[dy, 1], get("w1")[dy, 2]]
        wgt1[dy, 0:HALF, :] = jnp.concatenate([taps[1], taps[0]], axis=1)
        wgt1[dy, HALF : 2 * HALF, :] = jnp.concatenate([taps[2], taps[1]], axis=1)
        wgt1[dy, 2 * HALF : 3 * HALF, :] = jnp.concatenate([zero, taps[2]], axis=1)
        wgt1[dy, 3 * HALF :, :] = jnp.concatenate([taps[0], zero], axis=1)
    body1 = h1 * rows2
    native1 = h1 * PAIR
    buf1[0:rows2, :] = jnp.zeros((rows2, buf1.shape[1]), jnp.bfloat16)
    buf1[rows2 + body1 :, :] = jnp.zeros((rows2, buf1.shape[1]), jnp.bfloat16)
    for first in range(0, h1, group):
        lines = min(group, h1 - first)
        block = get("s1")[first * native1 : (first + lines) * native1, :]
        twice = jnp.concatenate([block, block], axis=1)
        lower = iota((lines * rows2, LANES), 1) < HALF
        moved = [dot(get("p1")[t, : lines * rows2, : lines * native1], twice) for t in range(PAIR)]
        start = (1 + first) * rows2
        stop = start + lines * rows2
        before, centre, after = neighbours(jnp.where(lower, moved[0], moved[1]))
        buf1[start:stop, 0:LANES] = centre.astype(jnp.bfloat16)
        buf1[start:stop, LANES:] = jnp.where(lower, after, before).astype(jnp.bfloat16)
    acc1 = None
    for dy in range(3):
        term = dot(buf1[dy * rows2 : dy * rows2 + body1, :], wgt1[dy])
        acc1 = term if acc1 is None else acc1 + term
    gain1 = jnp.concatenate([get("g1")[...], get("g1")[...]], axis=1)
    bias1 = jnp.concatenate([get("b1")[...], get("b1")[...]], axis=1)
    kept1[...] = keep(acc1, gain1, bias1)
    index_row = padded_index(get("index"))
    rank_col = column_of(rank_row(index_row))
    slot = iota((LANES, LANES), 1).astype(jnp.float32)
    ranked = jnp.sum(jnp.where(rank_col == slot, column_of(index_row), 0.0), axis=0, keepdims=True)
    ranked = ranked.astype(jnp.int32)
    ones = jnp.sum(jnp.where(index_row < base2, 1.0, 0.0))
    twos = jnp.sum(jnp.where(index_row < base3, 1.0, 0.0))
    small = (ones <= QUARTER) & (twos <= HALF)

    body2 = h2 * rows2
    native2 = h2 * PAIR
    buf2[0:rows2, :] = jnp.zeros((rows2, buf2.shape[1]), jnp.bfloat16)
    buf2[rows2 + body2 :, :] = jnp.zeros((rows2, buf2.shape[1]), jnp.bfloat16)
    for first in range(0, h2, group):
        lines = min(group, h2 - first)
        block = get("s2")[first * native2 : (first + lines) * native2, :]
        centre = dot(get("p2")[: lines * rows2, : lines * native2], block)
        start = (1 + first) * rows2
        for tap, moved in enumerate(neighbours(centre)):
            lanes = slice(tap * LANES, (tap + 1) * LANES)
            buf2[start : start + lines * rows2, lanes] = moved.astype(jnp.bfloat16)
    acc2 = None
    for dy in range(3):
        left = buf2[dy * rows2 : dy * rows2 + body2, :]
        term = dot(left, get("w2")[dy].reshape(3 * LANES, LANES))
        acc2 = term if acc2 is None else acc2 + term
    kept2[...] = keep(acc2, get("g2")[...], get("b2")[...])
    rows3 = pitch3 * PAIR
    body3 = h3 * rows3
    buf3[0:rows3, :] = jnp.zeros((rows3, buf3.shape[1]), jnp.bfloat16)
    buf3[rows3 + body3 :, :] = jnp.zeros((rows3, buf3.shape[1]), jnp.bfloat16)
    for y in range(h3):
        for x in range(h3):
            at = (y * h3 + x) * PAIR
            near3[at : at + PAIR, :] = get("s3")[y, x]
    third = near3[...]
    width3 = buf3.shape[1] // 3
    centre = dot(get("p3")[:, : third.shape[0]], third)
    for tap, moved in enumerate(neighbours(centre)):
        lanes = slice(tap * width3, (tap + 1) * width3)
        buf3[rows3 : rows3 + body3, lanes] = moved.astype(jnp.bfloat16)
    acc3 = None
    for dy in range(3):
        for tap in range(3):
            left = buf3[dy * rows3 : dy * rows3 + body3, tap * width3 : (tap + 1) * width3]
            term = dot(left, get("w3")[dy, tap])
            acc3 = term if acc3 is None else acc3 + term
    kept3[...] = keep(acc3, get("g3")[...], get("b3")[...])
    for name in list(copies):
        get(name)

    def picks(slots1, slots2, slots3, parts):
        half = iota((LANES, LANES), 0) // HALF == (iota((LANES, LANES), 1) // parts) % PAIR
        return (
            one_hot((slots1 == iota((LANES, LANES), 0) % HALF) & half),
            one_hot(slots2 == base2 + iota((LANES, slots2.shape[1]), 0)),
            one_hot(slots3 == base3 + iota((2 * LANES, slots3.shape[1]), 0)),
        )

    def repeated(first, width, times):
        row = jnp.concatenate([ranked[:, first : first + width]] * times, axis=1)
        room = -row.shape[1] % LANES
        return row if room == 0 else jnp.concatenate([row, jnp.full((1, room), -1, jnp.int32)], axis=1)

    def doubled(rows):
        shape = (h2, PAIR, rows2, LANES)
        return jnp.broadcast_to(rows.reshape(h2, 1, rows2, LANES), shape).reshape(body1, LANES)

    def flagged(rows, lane_is_flag):
        image = iota(rows.shape, 0) % PAIR
        return jnp.where(lane_is_flag, jnp.where(image < count, 1.0, 0.0), rows)

    lines = h1 // owners

    def each_owner(of_owner):
        for k in range(owners):
            owner = lax.axis_index("pos") ^ k
            of_owner(k, owner, pl.ds(pl.multiple_of(owner * (lines * rows2), rows2), lines * rows2))

    def coarse_rows(line, count_lines):
        return coarses[pl.ds(pl.multiple_of(line * rows2, rows2), count_lines * rows2), :]

    small_ref[0, 0] = jnp.where(small, 1, 0)

    @pl.when(jnp.logical_not(small))
    def _():
        low, high = repeated(0, HALF, 2), repeated(HALF, HALF, 2)
        both = jnp.concatenate([low, high], axis=1)
        pick1, pick2, pick3 = picks(low, both, both, HALF)
        chosen3 = dot(kept3[...], pick3).astype(jnp.bfloat16)
        coarse = dot(kept2[...], pick2) + dot(held["up"][:, :body3], chosen3)
        fines[...] = (dot(kept1[...], pick1) + doubled(coarse[:, :LANES])).astype(jnp.bfloat16)
        lane = iota((body2, LANES), 1)
        coarse = flagged(coarse[:, LANES:], lane % HALF == kept - HALF)
        coarses[...] = coarse.astype(jnp.bfloat16)

        def of_owner(k, owner, at):
            base = owner * lines // PAIR
            lower = iota((PAIR * rows2, LANES), 1) < HALF
            narrow = jnp.where(lower, coarse_rows(base, PAIR), coarse_rows(base + PAIR, PAIR))
            packed = dot(held["c1"][:, : lines * rows2], fines[at, :])
            packed = packed + dot(held["c2"][:, : PAIR * rows2], narrow)
            packed = packed.astype(jnp.bfloat16)
            tops[k][...] = packed[: tops[k].shape[0]]
            rests[k][...] = packed[tops[k].shape[0] :]

        each_owner(of_owner)

    @pl.when(small)
    def _():
        low, mid = repeated(0, QUARTER, 4), repeated(QUARTER, QUARTER, 4)
        high = repeated(HALF, THIRD, 3)
        pick1, pick2, pick3 = picks(
            low, jnp.concatenate([low, mid], axis=1), jnp.concatenate([low, mid, high], axis=1), QUARTER
        )
        chosen3 = dot(kept3[...], pick3)
        coarse = dot(kept2[...], pick2)
        coarse = coarse + dot(held["up"][:, :body3], chosen3[:, : 2 * LANES].astype(jnp.bfloat16))
        fines[...] = (dot(kept1[...], pick1) + doubled(coarse[:, :LANES])).astype(jnp.bfloat16)
        coarses[...] = coarse[:, LANES:].astype(jnp.bfloat16)
        lane = iota((body3, LANES), 1)
        third = flagged(chosen3[:, 2 * LANES :], lane % THIRD == kept - HALF)
        thirds[0:body3, :] = third.astype(jnp.bfloat16)
        thirds[body3:, :] = jnp.zeros((thirds.shape[0] - body3, LANES), jnp.bfloat16)

        def of_owner(k, owner, at):
            wide = fines[at, :]
            size = tops[k].shape[0]
            lane = iota((size, LANES), 1)
            packed = jnp.where(
                lane < HALF,
                dot(held["k1"][0, :, : lines * rows2], wide),
                dot(held["k1"][1, :, : lines * rows2], wide),
            )
            base = owner * lines // PAIR
            lane = iota((rows2, LANES), 1) // QUARTER
            middle = coarse_rows(base, 1)
            for level in range(1, 4):
                middle = jnp.where(lane == level, coarse_rows(base + level, 1), middle)
            base = owner * lines // 4
            lane = iota((rows3, LANES), 1) // THIRD
            far = None
            for level in range(3):
                line = thirds[pl.ds(pl.multiple_of((base + level) * rows3, rows3), rows3), :]
                far = line if far is None else jnp.where(lane == level, line, far)
            packed = packed + dot(held["k2"][:, :rows2], middle) + dot(held["k3"][:, :rows3], far)
            tops[k][...] = packed.astype(jnp.bfloat16)

        each_owner(of_owner)


def merge_kernel(*refs):
    *parts, out_ref = refs
    piece = 16
    size = piece * len(parts)
    to, source = iota((size, size), 0), iota((size, size), 1)
    each = len(parts) * PAIR
    wanted = (to % each) // PAIR * piece + (to // each) * PAIR + to % PAIR
    table = one_hot(source == wanted)
    for block in range(out_ref.shape[0] // size):
        rows = slice(block * piece, (block + 1) * piece)
        stack = jnp.concatenate([part[rows, :] for part in parts], axis=0)
        out_ref[block * size : (block + 1) * size, :] = dot(table, stack).astype(jnp.bfloat16)


def covariance_kernel(dims, *refs):
    shards, lines, columns, kept, depth, pairs, steps, small = dims
    idx_ref = refs[0]
    shard_refs = refs[1 : 1 + shards]
    mean_ref, cov_ref = refs[1 + shards : 3 + shards]
    packs, wide, table, eye, means, out, sems, *grams = refs[3 + shards :]
    images = packs.shape[1]
    each = images // shards
    fine = lines * columns
    block = cov_ref.shape[0]
    size = pairs * PAIR

    for j in range(shards):
        packs[:, j * each : (j + 1) * each, :] = shard_refs[j][...]
    rank = rank_row(padded_index(idx_ref)).astype(jnp.int32)
    rank = jnp.concatenate([rank, rank], axis=1)
    r = iota((LANES, 2 * LANES), 0)
    side = iota((LANES, 2 * LANES), 1) // LANES
    if small:
        levels = [
            (rank == r % QUARTER) & ((r // QUARTER) % PAIR == side),
            rank - QUARTER == r % QUARTER,
            (rank - HALF == r % THIRD) & (r < 3 * THIRD),
        ]
        levels[1] = levels[1] & (rank < HALF)
    else:
        levels = [(rank == r % HALF) & (r // HALF == side), rank - HALF == r % HALF]
    for n, level in enumerate(levels):
        table[n * LANES : (n + 1) * LANES, :] = one_hot(level)

    first_line = lines * lax.axis_index("pos")
    lane = iota((images, LANES), 1)

    def part(row, width=None, level=None):
        rows = packs[row]
        return rows if width is None else jnp.where(lane // width == level, rows, jnp.zeros_like(rows))

    def pack_of(at):
        line, column = at // columns, at % columns
        second = (line + first_line) // PAIR - first_line // PAIR
        if small:
            half = columns // PAIR
            third = (line + first_line) // 4 - first_line // 4
            found = [
                part(line * half + column // PAIR, HALF, column % PAIR),
                part(lines * half + column, QUARTER, second),
                part(lines * half + columns + column // PAIR, THIRD, third),
            ]
        else:
            found = [part(at), part(fine + (second % PAIR) * columns + column, HALF, second // PAIR)]
        return jnp.concatenate(found, axis=1)

    square = (depth, LANES)
    eye[...] = jnp.where(iota(square, 0) == iota(square, 1), 0.01, 0.0)

    def products(step, into):
        first = step * pairs
        rows = [pack_of(first + t) for t in range(pairs)]
        values = dot(jnp.concatenate(rows, axis=0), table[...])
        wide[...] = values.astype(jnp.bfloat16)

        sums = jnp.sum(values.reshape(pairs, images, 2 * LANES), axis=1)
        total = sums[0:1, kept : kept + 1]
        mean = sums / total
        inverse = jnp.broadcast_to(1.0 / (total - 1.0), (1, LANES))
        a, b, c = pieces(sums)
        d, e, f = pieces(-mean)
        row = iota((16, 2 * LANES), 0)
        zero = jnp.zeros((images + 16, LANES), jnp.bfloat16)
        for t in range(pairs):
            at = slice(t, t + 1)
            third = jnp.where(row == 5, c[at], 0.0)
            left = jnp.where(row < 3, a[at], jnp.where(row < 5, b[at], third))
            third = jnp.where(row == 2, f[at], 0.0)
            right = jnp.where((row == 1) | (row == 4), e[at], third)
            right = jnp.where((row == 0) | (row == 3) | (row == 5), d[at], right)
            left, right = left.astype(jnp.bfloat16), right.astype(jnp.bfloat16)
            pair = wide[t * images : (t + 1) * images, :]
            even, other = pair[:, :LANES], pair[:, LANES:]
            stack = jnp.concatenate([even, left[:, :LANES], other, left[:, LANES:]], axis=0)
            even = jnp.concatenate([even, right[:, :LANES]], axis=0)
            other = jnp.concatenate([other, right[:, LANES:]], axis=0)
            block = jnp.concatenate(
                [
                    jnp.concatenate([even, zero], axis=1),
                    jnp.concatenate([zero, other], axis=1),
                ],
                axis=0,
            )
            moment = lax.dot_general(
                stack, block, (((0,), (0,)), ((), ())), preferred_element_type=jnp.float32
            )
            for side in range(PAIR):
                position = t * PAIR + side
                half = slice(side * LANES, (side + 1) * LANES)
                means[pl.ds(step * size + position, 1), :] = mean[at, half]
                start = (position % 8) * depth
                value = moment[:depth, half] * inverse + eye[...]
                into[position // 8][start : start + depth, :] = value

    def copy_out(step, count):
        rows = pl.ds(step * size if isinstance(step, int) else pl.multiple_of(step * size, size), count)
        return pltpu.make_async_copy(out.at[rows], cov_ref.at[rows], sems.at[step])

    def rows_out(step, source, count):
        for part, gram in enumerate(source):
            at = step * size + part * 8
            rows = pl.ds(at if isinstance(at, int) else pl.multiple_of(at, 8), 8)
            for k in range(kept):
                value = gram[pl.ds(k, 8, stride=depth), :]
                out[rows, k * kept : (k + 1) * kept] = value[:, :kept]
        copy_out(step, count).start()

    ready, coming = grams[: len(grams) // 2], grams[len(grams) // 2 :]
    tail = block - (steps - 1) * size
    products(0, ready)

    def two_steps(i, carry):
        products(2 * i + 1, coming)
        rows_out(2 * i, ready, size)
        products(2 * i + 2, ready)
        rows_out(2 * i + 1, coming, size)
        return carry

    lax.fori_loop(0, (steps - 1) // 2, two_steps, 0)
    if steps % 2 == 0:
        products(steps - 1, coming)
        rows_out(steps - 2, ready, size)
        ready = coming
    rows_out(steps - 1, ready, tail)
    mean_ref[...] = means[:block, :kept]
    for step in range(steps):
        copy_out(step, size if step < steps - 1 else tail).wait()


def shift_tables(h1, h2, h3, owners, group, pitch2, pitch3):
    rows2 = pitch2 * PAIR
    p1 = np.zeros((PAIR, group * rows2, group * h1 * PAIR), np.float32)
    p2 = np.zeros((group * rows2, group * h2 * PAIR), np.float32)
    for y in range(group):
        for x in range(h2):
            for i in range(PAIR):
                to = y * rows2 + x * PAIR + i
                for t in range(PAIR):
                    p1[t, to, (y * h1 + 2 * x + t) * PAIR + i] = 1
                p2[to, (y * h2 + x) * PAIR + i] = 1
    p3 = np.zeros((h3 * pitch3 * PAIR, h3 * h3 * PAIR), np.float32)
    for y in range(h3):
        for x in range(h3):
            for i in range(PAIR):
                p3[(y * pitch3 + x) * PAIR + i, (y * h3 + x) * PAIR + i] = 1
    up = np.zeros((h2 * rows2, h3 * pitch3 * PAIR), np.float32)
    for y in range(h2):
        for x in range(h2):
            for i in range(PAIR):
                up[y * rows2 + x * PAIR + i, ((y // 2) * pitch3 + x // 2) * PAIR + i] = 1
    lines = h1 // owners
    packed = pack_rows(h1, owners)
    c1 = np.zeros((packed, lines * rows2), np.float32)
    c2 = np.zeros((packed, PAIR * rows2), np.float32)
    for x in range(h2):
        for i in range(PAIR):
            for y in range(lines):
                c1[(y * h2 + x) * PAIR + i, y * rows2 + x * PAIR + i] = 1
            for y in range(PAIR):
                c2[((lines + y) * h2 + x) * PAIR + i, y * rows2 + x * PAIR + i] = 1
    small = small_rows(h1, owners)
    half = h2 // PAIR
    k1 = np.zeros((PAIR, small, lines * rows2), np.float32)
    k2 = np.zeros((small, rows2), np.float32)
    k3 = np.zeros((small, pitch3 * PAIR), np.float32)
    for i in range(PAIR):
        for x in range(half):
            for y in range(lines):
                for q in range(PAIR):
                    k1[q, (y * half + x) * PAIR + i, y * rows2 + (PAIR * x + q) * PAIR + i] = 1
            k3[(lines * half + h2 + x) * PAIR + i, x * PAIR + i] = 1
        for x in range(h2):
            k2[(lines * half + x) * PAIR + i, x * PAIR + i] = 1
    tables = []
    for a in (p1, p2, p3, up, c1, c2, k1, k2, k3):
        room = [(0, 0)] * (a.ndim - 1) + [(0, -a.shape[-1] % LANES)]
        tables.append(jnp.asarray(np.pad(a, room), jnp.bfloat16))
    return tables


def pack_rows(h1, owners):
    lines = h1 // owners
    rows = (lines + PAIR) * (h1 // 2) * PAIR
    return -(-rows // 16) * 16


def small_rows(h1, owners):
    half = h1 // 4
    rows = (h1 // owners * half + 3 * half) * PAIR
    return -(-rows // 16) * 16


def packed_path(
    section_one,
    section_two,
    section_three,
    weight_one,
    weight_two,
    weight_three,
    gain_one,
    gain_two,
    gain_three,
    bias_one,
    bias_two,
    bias_three,
    channel_index,
    valid_count,
):
    slots, h1 = section_one.shape[:2]
    h2, h3 = section_two.shape[1], section_three.shape[1]
    c1, c2, c3 = section_one.shape[3], section_two.shape[3], section_three.shape[3]
    kept = channel_index.shape[0]
    owners = lax.axis_size("pos")
    groups = lax.axis_size("img")
    group, pitch2, pitch3 = 4, 16, 8
    tables = shift_tables(h1, h2, h3, owners, group, pitch2, pitch3)
    packed = pack_rows(h1, owners)
    rows2, rows3 = pitch2 * PAIR, pitch3 * PAIR

    def flat(section):
        return jnp.transpose(section, (1, 2, 0, 3)).reshape(-1, section.shape[3])

    index = channel_index.reshape(1, kept)
    smem = pl.BlockSpec(memory_space=pltpu.SMEM)
    vmem = pl.BlockSpec(memory_space=pltpu.VMEM)
    third = jnp.transpose(section_three, (1, 2, 0, 3))
    p1, p2, p3, up, *packing = tables
    operands = [
        *(flat(section_one), p1, weight_one, gain_one.reshape(1, c1), bias_one.reshape(1, c1)),
        index,
        *(flat(section_two), p2, weight_two, gain_two.reshape(1, c2), bias_two.reshape(1, c2)),
        *(third, p3, weight_three, gain_three.reshape(1, c3), bias_three.reshape(1, c3)),
        *(up, *packing),
    ]
    top = small_rows(h1, owners)
    shapes = [(top, LANES)] * owners + [(packed - top, LANES)] * owners
    *packs, small = pl.pallas_call(
        functools.partial(features_kernel, (h1, h2, h3, owners, kept, group, pitch2, pitch3)),
        out_shape=[jax.ShapeDtypeStruct(s, jnp.bfloat16) for s in shapes]
        + [jax.ShapeDtypeStruct((1, 1), jnp.int32)],
        in_specs=[pl.BlockSpec(memory_space=pl.ANY)] * len(operands) + [smem],
        out_specs=[pl.BlockSpec(s, lambda: (0, 0)) for s in shapes] + [smem],
        scratch_shapes=[
            pltpu.VMEM(((h1 + 2) * rows2, 2 * LANES), jnp.bfloat16),
            pltpu.VMEM(((h2 + 2) * rows2, 3 * LANES), jnp.bfloat16),
            pltpu.VMEM(((h3 + 2) * rows3, 3 * c3), jnp.bfloat16),
            pltpu.VMEM((h3 * h3 * PAIR, c3), jnp.bfloat16),
            pltpu.VMEM((3, 2 * LANES, LANES), jnp.bfloat16),
            pltpu.VMEM((h1 * rows2, LANES), jnp.bfloat16),
            pltpu.VMEM((h2 * rows2, LANES), jnp.bfloat16),
            pltpu.VMEM((h3 * rows3, c3), jnp.bfloat16),
            pltpu.VMEM((h1 * rows2, LANES), jnp.bfloat16),
            pltpu.VMEM((h2 * rows2, LANES), jnp.bfloat16),
            pltpu.VMEM(((h3 + 1) * rows3, LANES), jnp.bfloat16),
            pltpu.SemaphoreType.DMA((len(operands),)),
        ]
        + [pltpu.VMEM(a.shape, a.dtype) for a in operands],
        name="features",
    )(*operands, valid_count)
    sizes = (slots, h1, h2, kept, owners, groups)

    def small_packs(index, *packs):
        return finish(sizes, True, index, packs[:owners])

    def large_packs(index, *packs):
        full = [jnp.concatenate(p, axis=0) for p in zip(packs[:owners], packs[owners:])]
        return finish(sizes, False, index, full)

    mean, covariance = lax.cond(small[0, 0] > 0, small_packs, large_packs, index, *packs)
    return mean.T, covariance


def finish(sizes, small, index, packs):
    slots, h1, h2, kept, owners, groups = sizes
    packed = packs[0].shape[0]
    vmem = pl.BlockSpec(memory_space=pltpu.VMEM)

    parts = [packs[0]]
    for k in range(1, owners):
        pairs = [(i, i ^ k) for i in range(owners)]
        parts.append(lax.ppermute(packs[k], "pos", pairs))
    merged_shape = jax.ShapeDtypeStruct((packed * owners, LANES), jnp.bfloat16)
    merged = pl.pallas_call(
        merge_kernel,
        out_shape=merged_shape,
        in_specs=[vmem] * owners,
        out_specs=vmem,
        compiler_params=pltpu.CompilerParams(vmem_limit_bytes=8 << 20),
        name="merge",
    )(*parts)

    levels = groups // PAIR
    shards = [merged]
    turns = sorted(range(1, levels), key=lambda t: (min(t, levels - t), t))
    for turn in turns:
        pairs = [
            (z * PAIR + c, ((z + turn) % levels) * PAIR + c)
            for z in range(levels)
            for c in range(PAIR)
        ]
        shards.append(lax.ppermute(merged, "img", pairs))
    swap = [(i, i ^ 1) for i in range(groups)]
    shards = shards + [lax.ppermute(s, "img", swap) for s in shards]

    lines, columns = h1 // owners, h2
    block = lines * h1
    each = owners * slots
    images = each * len(shards)
    shards = [s.reshape(packed // PAIR, each, LANES) for s in shards]
    parts = 2
    steps = -(-block // (8 * parts))
    depth = -(-(kept + 1) // 8) * 8
    pairs = 4 * parts
    size = 8 * parts
    mean_shape = jax.ShapeDtypeStruct((block, kept), jnp.float32)
    mean, covariance = pl.pallas_call(
        functools.partial(
            covariance_kernel, (len(shards), lines, columns, kept, depth, pairs, steps, small)
        ),
        out_shape=(mean_shape, jax.ShapeDtypeStruct((block, kept * kept), jnp.float32)),
        in_specs=[vmem] * (1 + len(shards)),
        out_specs=(vmem, pl.BlockSpec(memory_space=pl.ANY)),
        compiler_params=pltpu.CompilerParams(vmem_limit_bytes=24 << 20),
        scratch_shapes=[
            pltpu.VMEM((packed // PAIR, images, LANES), jnp.bfloat16),
            pltpu.VMEM((pairs * images, 2 * LANES), jnp.bfloat16),
            pltpu.VMEM(((3 if small else 2) * LANES, 2 * LANES), jnp.bfloat16),
            pltpu.VMEM((depth, LANES), jnp.float32),
            pltpu.VMEM((steps * size, LANES), jnp.float32),
            pltpu.VMEM((steps * size, kept * kept), jnp.float32),
            pltpu.SemaphoreType.DMA((steps,)),
        ]
        + [pltpu.VMEM((8 * depth, LANES), jnp.float32) for _ in range(2 * parts)],
        name="covariance",
    )(index, *shards)
    return mean, covariance


def suits(mesh, section_one, section_two, section_three, channel_index):
    owners, groups = mesh.shape["pos"], mesh.shape["img"]
    devices = owners * groups
    images, h1, _, c1 = section_one.shape
    h2, c2 = section_two.shape[1], section_two.shape[3]
    h3, c3 = section_three.shape[1], section_three.shape[3]
    kept = channel_index.shape[0]
    lines = h1 // owners
    return (
        images == PAIR * devices
        and owners == 4
        and groups % PAIR == 0
        and h1 % owners == 0
        and h1 == 2 * h2 == 4 * h3
        and h2 <= 16
        and h3 <= 8
        and (c1, c2, c3) == (HALF, LANES, 2 * LANES)
        and HALF <= kept < LANES
        and kept - HALF < THIRD
        and lines == 7
    )


def solution(mesh):
    in_specs = (
        P(("img", "pos"), None, None, None),
        P(("img", "pos"), None, None, None),
        P(("img", "pos"), None, None, None),
        P(),
        P(),
        P(),
        P(),
        P(),
        P(),
        P(),
        P(),
        P(),
        P(),
        P("img", "pos"),
    )

    def run(*arrays):
        chosen = suits(mesh, arrays[0], arrays[1], arrays[2], arrays[12])
        return jax.shard_map(
            packed_path if chosen else plain,
            mesh=mesh,
            in_specs=in_specs,
            out_specs=(P(None, "pos"), P("pos", None)),
            check_vma=False,
        )(*arrays)

    return run
```

```python
import functools

import jax
import jax.numpy as jnp
import numpy as np
from jax import lax
from jax.experimental import pallas as pl
from jax.experimental.pallas import tpu as pltpu
from jax.sharding import PartitionSpec as P


LANES = 128
HALF = 64
THIRD = 42
QUARTER = 32
PAIR = 2


def section_out(images, weight, gain, bias):
    conv = lax.conv_general_dilated(
        images,
        weight,
        (1, 1),
        "SAME",
        dimension_numbers=("NHWC", "HWIO", "NHWC"),
        preferred_element_type=jnp.float32,
    )
    return jax.nn.relu(conv * gain + bias).astype(jnp.bfloat16)


def pick_channels(section, offset, width, channel_index):
    table = (channel_index[None, :] - offset == lax.iota(jnp.int32, width)[:, None]).astype(
        jnp.bfloat16
    )
    return jnp.einsum("ihwc,ck->ikhw", section, table, preferred_element_type=jnp.float32).astype(
        jnp.bfloat16
    )


def widen(picked, factor):
    return jnp.repeat(jnp.repeat(picked, factor, axis=2), factor, axis=3)


def pair_outer(rows):
    return (rows[:, :, None] * rows[:, None, :]).reshape(
        rows.shape[0], rows.shape[1] * rows.shape[1]
    )


def product_rows(values):
    kept = values.shape[1]
    raw = jnp.einsum("ikp,ilp->pkl", values, values, preferred_element_type=jnp.float32)
    return raw.reshape(values.shape[2], kept * kept)


def plain(
    section_one,
    section_two,
    section_three,
    weight_one,
    weight_two,
    weight_three,
    gain_one,
    gain_two,
    gain_three,
    bias_one,
    bias_two,
    bias_three,
    channel_index,
    valid_count,
):
    slots = section_one.shape[0]
    side = section_one.shape[1]
    width_one = section_one.shape[3]
    width_two = section_two.shape[3]
    width_three = section_three.shape[3]
    kept = channel_index.shape[0]
    owners = lax.axis_size("pos")
    block = side * side // owners
    own_count = valid_count[0, 0]
    scale = (lax.iota(jnp.int32, slots) < own_count).astype(jnp.bfloat16)[:, None, None, None]
    out_one = section_out(section_one, weight_one, gain_one, bias_one) * scale
    out_two = section_out(section_two, weight_two, gain_two, bias_two) * scale
    out_three = section_out(section_three, weight_three, gain_three, bias_three) * scale
    features = pick_channels(out_one, 0, width_one, channel_index)
    features = features + widen(pick_channels(out_two, width_one, width_two, channel_index), 2)
    features = features + widen(
        pick_channels(out_three, width_one + width_two, width_three, channel_index), 4
    )
    shaped = features.reshape(slots, kept, owners, block)
    group = lax.psum(own_count, "pos").astype(jnp.float32)
    owned = lax.all_to_all(shaped, "pos", split_axis=2, concat_axis=0, tiled=True)[:, :, 0, :]
    values = lax.all_gather(owned, "img", axis=0, tiled=True)
    counts = lax.all_gather(group.astype(jnp.bfloat16)[None], "img", axis=0, tiled=True)
    total = jnp.sum(counts.astype(jnp.float32))
    all_sums = jnp.sum(values, axis=0, dtype=jnp.float32).T
    all_raw = product_rows(values)
    mean = all_sums / total
    moment = all_raw - total * pair_outer(mean)
    covariance = moment / (total - 1.0) + 0.01 * jnp.eye(kept, dtype=jnp.float32).reshape(
        1, kept * kept
    )
    return (mean.T, covariance)


def dot(a, b):
    return lax.dot_general(a, b, (((1,), (0,)), ((), ())), preferred_element_type=jnp.float32)


def iota(shape, dim):
    return lax.broadcasted_iota(jnp.int32, shape, dim)


def padded_index(idx_ref):
    kept = idx_ref.shape[1]
    lane = iota((1, LANES), 1)
    row = jnp.concatenate([idx_ref[...], jnp.zeros((1, LANES - kept), jnp.int32)], axis=1)
    return jnp.where(lane < kept, row, 100000 + lane).astype(jnp.float32)


def column_of(row):
    spread = jnp.broadcast_to(row, (LANES, LANES))
    diagonal = iota((LANES, LANES), 0) == iota((LANES, LANES), 1)
    return jnp.sum(jnp.where(diagonal, spread, 0.0), axis=1, keepdims=True)


def rank_row(idx_row):
    smaller = column_of(idx_row) < idx_row
    return jnp.sum(jnp.where(smaller, 1.0, 0.0), axis=0, keepdims=True)


def one_hot(mask):
    return jnp.where(mask, 1.0, 0.0).astype(jnp.bfloat16)


def pieces(values):
    found = []
    for _ in range(3):
        piece = values.astype(jnp.bfloat16).astype(jnp.float32)
        found.append(piece)
        values = values - piece
    return found


def neighbours(rows):
    count = rows.shape[0]
    return pltpu.roll(rows, PAIR, 0), rows, pltpu.roll(rows, count - PAIR, 0)


def features_kernel(dims, *refs):
    names = "s1 p1 w1 g1 b1 index s2 p2 w2 g2 b2 s3 p3 w3 g3 b3 up c1 c2 k1 k2 k3".split()
    given = refs[: len(names) + 1]
    count_ref = given[-1]
    tops, rests, small_ref = refs[len(given) :][: dims[3]], refs[len(given) + dims[3] :][: dims[3]], refs[len(given) + 2 * dims[3]]
    scratch = refs[len(given) + 2 * dims[3] + 1 :]
    buf1, buf2, buf3, near3, wgt1, kept1, kept2, kept3, fines, coarses, thirds, sems = scratch[:12]
    held = dict(zip(names, scratch[12:]))
    copies = {}
    for n, name in enumerate(names):
        copies[name] = pltpu.make_async_copy(given[n], held[name], sems.at[n])
        copies[name].start()

    def get(name):
        if name in copies:
            copies.pop(name).wait()
        return held[name]

    h1, h2, h3, owners, kept, group, pitch2, pitch3 = dims
    count = count_ref[0, 0]
    base2, base3 = HALF, HALF + LANES

    def keep(values, gain, bias):
        image = iota((values.shape[0], 1), 0) % PAIR
        shaped = jnp.maximum(values * gain + bias, 0.0)
        return jnp.where(image < count, shaped, 0.0).astype(jnp.bfloat16)

    for name in list(copies):
        get(name)
    rows2 = pitch2 * PAIR
    zero = jnp.zeros((HALF, HALF), jnp.bfloat16)
    for dy in range(3):
        taps = [get("w1")[dy, 0], get("w1")[dy, 1], get("w1")[dy, 2]]
        wgt1[dy, 0:HALF, :] = jnp.concatenate([taps[1], taps[0]], axis=1)
        wgt1[dy, HALF : 2 * HALF, :] = jnp.concatenate([taps[2], taps[1]], axis=1)
        wgt1[dy, 2 * HALF : 3 * HALF, :] = jnp.concatenate([zero, taps[2]], axis=1)
        wgt1[dy, 3 * HALF :, :] = jnp.concatenate([taps[0], zero], axis=1)
    body1 = h1 * rows2
    native1 = h1 * PAIR
    buf1[0:rows2, :] = jnp.zeros((rows2, buf1.shape[1]), jnp.bfloat16)
    buf1[rows2 + body1 :, :] = jnp.zeros((rows2, buf1.shape[1]), jnp.bfloat16)
    for first in range(0, h1, group):
        lines = group
        block = get("s1")[first * native1 : (first + lines) * native1, :]
        twice = jnp.concatenate([block, block], axis=1)
        lower = iota((lines * rows2, LANES), 1) < HALF
        moved = dot(get("p1")[:, : lines * native1], twice)
        start = (1 + first) * rows2
        stop = start + lines * rows2
        half = lines * rows2
        before, centre, after = neighbours(jnp.where(lower, moved[:half], moved[half:]))
        buf1[start:stop, 0:LANES] = centre.astype(jnp.bfloat16)
        buf1[start:stop, LANES:] = jnp.where(lower, after, before).astype(jnp.bfloat16)
    left = [buf1[dy * rows2 : dy * rows2 + body1, :] for dy in range(3)]
    acc1 = dot(jnp.concatenate(left, axis=1), wgt1[...].reshape(3 * 2 * LANES, LANES))
    gain1 = jnp.concatenate([get("g1")[...], get("g1")[...]], axis=1)
    bias1 = jnp.concatenate([get("b1")[...], get("b1")[...]], axis=1)
    kept1[...] = keep(acc1, gain1, bias1)
    index_row = padded_index(get("index"))
    rank_col = column_of(rank_row(index_row))
    slot = iota((LANES, LANES), 1).astype(jnp.float32)
    ranked = jnp.sum(jnp.where(rank_col == slot, column_of(index_row), 0.0), axis=0, keepdims=True)
    ranked = ranked.astype(jnp.int32)
    ones = jnp.sum(jnp.where(index_row < base2, 1.0, 0.0))
    twos = jnp.sum(jnp.where(index_row < base3, 1.0, 0.0))
    small = (ones <= QUARTER) & (twos <= HALF)

    body2 = h2 * rows2
    native2 = h2 * PAIR
    buf2[0:rows2, :] = jnp.zeros((rows2, buf2.shape[1]), jnp.bfloat16)
    buf2[rows2 + body2 :, :] = jnp.zeros((rows2, buf2.shape[1]), jnp.bfloat16)
    for first in range(0, h2, group):
        lines = min(group, h2 - first)
        block = get("s2")[first * native2 : (first + lines) * native2, :]
        centre = dot(get("p2")[: lines * rows2, : lines * native2], block)
        start = (1 + first) * rows2
        for tap, moved in enumerate(neighbours(centre)):
            lanes = slice(tap * LANES, (tap + 1) * LANES)
            buf2[start : start + lines * rows2, lanes] = moved.astype(jnp.bfloat16)
    left = [buf2[dy * rows2 : dy * rows2 + body2, :] for dy in range(3)]
    acc2 = dot(jnp.concatenate(left, axis=1), get("w2")[...].reshape(9 * LANES, LANES))
    kept2[...] = keep(acc2, get("g2")[...], get("b2")[...])
    rows3 = pitch3 * PAIR
    body3 = h3 * rows3
    buf3[0:rows3, :] = jnp.zeros((rows3, buf3.shape[1]), jnp.bfloat16)
    buf3[rows3 + body3 :, :] = jnp.zeros((rows3, buf3.shape[1]), jnp.bfloat16)
    for y in range(h3):
        for x in range(h3):
            at = (y * h3 + x) * PAIR
            near3[at : at + PAIR, :] = get("s3")[y, x]
    third = near3[...]
    width3 = buf3.shape[1] // 3
    centre = dot(get("p3")[:, : third.shape[0]], third)
    for tap, moved in enumerate(neighbours(centre)):
        lanes = slice(tap * width3, (tap + 1) * width3)
        buf3[rows3 : rows3 + body3, lanes] = moved.astype(jnp.bfloat16)
    left = [buf3[dy * rows3 : dy * rows3 + body3, :] for dy in range(3)]
    acc3 = dot(jnp.concatenate(left, axis=1), get("w3")[...].reshape(9 * width3, width3))
    kept3[...] = keep(acc3, get("g3")[...], get("b3")[...])
    for name in list(copies):
        get(name)

    def picks(slots1, slots2, slots3, parts):
        half = iota((LANES, LANES), 0) // HALF == (iota((LANES, LANES), 1) // parts) % PAIR
        return (
            one_hot((slots1 == iota((LANES, LANES), 0) % HALF) & half),
            one_hot(slots2 == base2 + iota((LANES, slots2.shape[1]), 0)),
            one_hot(slots3 == base3 + iota((2 * LANES, slots3.shape[1]), 0)),
        )

    def repeated(first, width, times):
        row = jnp.concatenate([ranked[:, first : first + width]] * times, axis=1)
        room = -row.shape[1] % LANES
        return row if room == 0 else jnp.concatenate([row, jnp.full((1, room), -1, jnp.int32)], axis=1)

    def doubled(rows):
        shape = (h2, PAIR, rows2, LANES)
        return jnp.broadcast_to(rows.reshape(h2, 1, rows2, LANES), shape).reshape(body1, LANES)

    def flagged(rows, lane_is_flag):
        image = iota(rows.shape, 0) % PAIR
        return jnp.where(lane_is_flag, jnp.where(image < count, 1.0, 0.0), rows)

    lines = h1 // owners

    def each_owner(of_owner):
        for k in range(owners):
            owner = lax.axis_index("pos") ^ k
            of_owner(k, owner, pl.ds(pl.multiple_of(owner * (lines * rows2), rows2), lines * rows2))

    def coarse_rows(line, count_lines):
        return coarses[pl.ds(pl.multiple_of(line * rows2, rows2), count_lines * rows2), :]

    small_ref[0, 0] = jnp.where(small, 1, 0)

    @pl.when(jnp.logical_not(small))
    def _():
        low, high = repeated(0, HALF, 2), repeated(HALF, HALF, 2)
        both = jnp.concatenate([low, high], axis=1)
        pick1, pick2, pick3 = picks(low, both, both, HALF)
        chosen3 = dot(kept3[...], pick3).astype(jnp.bfloat16)
        coarse = dot(kept2[...], pick2) + dot(held["up"][:, :body3], chosen3)
        fines[...] = (dot(kept1[...], pick1) + doubled(coarse[:, :LANES])).astype(jnp.bfloat16)
        lane = iota((body2, LANES), 1)
        coarse = flagged(coarse[:, LANES:], lane % HALF == kept - HALF)
        coarses[...] = coarse.astype(jnp.bfloat16)

        def of_owner(k, owner, at):
            base = owner * lines // PAIR
            lower = iota((PAIR * rows2, LANES), 1) < HALF
            narrow = jnp.where(lower, coarse_rows(base, PAIR), coarse_rows(base + PAIR, PAIR))
            packed = dot(held["c1"][:, : lines * rows2], fines[at, :])
            packed = packed + dot(held["c2"][:, : PAIR * rows2], narrow)
            packed = packed.astype(jnp.bfloat16)
            tops[k][...] = packed[: tops[k].shape[0]]
            rests[k][...] = packed[tops[k].shape[0] :]

        each_owner(of_owner)

    @pl.when(small)
    def _():
        low, mid = repeated(0, QUARTER, 4), repeated(QUARTER, QUARTER, 4)
        high = repeated(HALF, THIRD, 3)
        pick1, pick2, pick3 = picks(
            low, jnp.concatenate([low, mid], axis=1), jnp.concatenate([low, mid, high], axis=1), QUARTER
        )
        chosen3 = dot(kept3[...], pick3)
        coarse = dot(kept2[...], pick2)
        coarse = coarse + dot(held["up"][:, :body3], chosen3[:, : 2 * LANES].astype(jnp.bfloat16))
        fines[...] = (dot(kept1[...], pick1) + doubled(coarse[:, :LANES])).astype(jnp.bfloat16)
        coarses[...] = coarse[:, LANES:].astype(jnp.bfloat16)
        lane = iota((body3, LANES), 1)
        third = flagged(chosen3[:, 2 * LANES :], lane % THIRD == kept - HALF)
        thirds[0:body3, :] = third.astype(jnp.bfloat16)
        thirds[body3:, :] = jnp.zeros((thirds.shape[0] - body3, LANES), jnp.bfloat16)

        def of_owner(k, owner, at):
            wide = fines[at, :]
            size = tops[k].shape[0]
            lane = iota((size, LANES), 1)
            moved = dot(held["k1"][:, : lines * rows2], wide)
            packed = jnp.where(lane < HALF, moved[:size], moved[size:])
            base = owner * lines // PAIR
            lane = iota((rows2, LANES), 1) // QUARTER
            middle = coarse_rows(base, 1)
            for level in range(1, 4):
                middle = jnp.where(lane == level, coarse_rows(base + level, 1), middle)
            base = owner * lines // 4
            lane = iota((rows3, LANES), 1) // THIRD
            far = None
            for level in range(3):
                line = thirds[pl.ds(pl.multiple_of((base + level) * rows3, rows3), rows3), :]
                far = line if far is None else jnp.where(lane == level, line, far)
            packed = packed + dot(held["k2"][:, :rows2], middle) + dot(held["k3"][:, :rows3], far)
            tops[k][...] = packed.astype(jnp.bfloat16)

        each_owner(of_owner)


def merge_kernel(*refs):
    *parts, out = refs
    owners = len(parts)
    piece = 16
    size = piece * owners
    to, source = iota((size, size), 0), iota((size, size), 1)
    each = owners * PAIR
    wanted = (to % each) // PAIR * piece + (to // each) * PAIR + to % PAIR
    table = one_hot(source == wanted)
    for block in range(out.shape[0] // size):
        rows = slice(block * piece, (block + 1) * piece)
        stack = jnp.concatenate([part[rows, :] for part in parts], axis=0)
        out[block * size : (block + 1) * size, :] = dot(table, stack).astype(jnp.bfloat16)


def covariance_kernel(dims, *refs):
    shards, lines, columns, kept, depth, pairs, small = dims
    idx_ref = refs[0]
    shard_refs = refs[1 : 1 + shards]
    mean_ref, cov_ref = refs[1 + shards : 3 + shards]
    packs, wide, table, eye, means, out, sems, coarse, *grams = refs[3 + shards :]
    block = cov_ref.shape[0]
    size = pairs * PAIR
    steps = -(-block // size)
    images = packs.shape[1]
    each = images // shards
    fine = lines * columns
    half = columns // PAIR

    for j in range(shards):
        packs[:, j * each : (j + 1) * each, :] = shard_refs[j][...]
    rank1 = rank_row(padded_index(idx_ref)).astype(jnp.int32)
    rank = jnp.concatenate([rank1, rank1], axis=1)
    r = iota((LANES, 2 * LANES), 0)
    side = iota((LANES, 2 * LANES), 1) // LANES
    first_line = lines * lax.axis_index("pos")
    lane = iota((images, LANES), 1)

    def part(rows, width, level):
        return jnp.where(lane // width == level, rows, jnp.zeros_like(rows))

    if small:
        table[...] = one_hot((rank == r % QUARTER) & ((r // QUARTER) % PAIR == side))
        ahead = columns + half
        r = iota((LANES, LANES), 0)
        levels = [
            one_hot((rank1 - QUARTER == r % QUARTER) & (rank1 < HALF)),
            one_hot((rank1 - HALF == r % THIRD) & (r < 3 * THIRD)),
        ]
        below = jnp.concatenate(levels, axis=0)
        for second in range(coarse.shape[0] // columns):
            third = (second + first_line // PAIR) // PAIR - first_line // 4
            rows = []
            for column in range(columns):
                far = part(packs[columns + column // PAIR], THIRD, third)
                rows.append(jnp.concatenate([part(packs[column], QUARTER, second), far], axis=1))
            values = dot(jnp.concatenate(rows, axis=0), below).astype(jnp.bfloat16)
            at = slice(second * columns, (second + 1) * columns)
            coarse[at] = values.reshape(columns, images, LANES)
    else:
        table[0:LANES, :] = one_hot((rank == r % HALF) & (r // HALF == side))
        table[LANES:, :] = one_hot(rank - HALF == r % HALF)

    def expanded(first):
        rows, more = [], []
        for t in range(pairs):
            at = first + t
            line, column = at // columns, at % columns
            second = (line + first_line) // PAIR - first_line // PAIR
            if small:
                row = jnp.minimum(ahead + at // PAIR, packs.shape[0] - 1)
                rows.append(part(packs[row], HALF, at % PAIR))
                more.append(coarse[jnp.minimum(second, 3) * columns + column])
            else:
                narrow = packs[fine + (second % PAIR) * columns + column]
                narrow = part(narrow, HALF, second // PAIR)
                rows.append(jnp.concatenate([packs[at], narrow], axis=1))
        values = dot(jnp.concatenate(rows, axis=0), table[...])
        if small:
            added = jnp.concatenate(more, axis=0).astype(jnp.float32)
            values = values + jnp.concatenate([added, added], axis=1)
        return values

    square = (depth, LANES)
    eye[...] = jnp.where(iota(square, 0) == iota(square, 1), 0.01, 0.0)

    def products(step, into):
        values = expanded(step * pairs)
        wide[...] = values.astype(jnp.bfloat16)

        sums = jnp.sum(values.reshape(pairs, images, 2 * LANES), axis=1)
        total = sums[0:1, kept : kept + 1]
        mean = sums / total
        inverse = jnp.broadcast_to(1.0 / (total - 1.0), (1, LANES))
        a, b, c = pieces(sums)
        d, e, f = pieces(-mean)
        row = iota((16, 2 * LANES), 0)
        zero = jnp.zeros((images + 16, LANES), jnp.bfloat16)
        for t in range(pairs):
            at = slice(t, t + 1)
            third = jnp.where(row == 5, c[at], 0.0)
            left = jnp.where(row < 3, a[at], jnp.where(row < 5, b[at], third))
            third = jnp.where(row == 2, f[at], 0.0)
            right = jnp.where((row == 1) | (row == 4), e[at], third)
            right = jnp.where((row == 0) | (row == 3) | (row == 5), d[at], right)
            left, right = left.astype(jnp.bfloat16), right.astype(jnp.bfloat16)
            pair = wide[t * images : (t + 1) * images, :]
            even, other = pair[:, :LANES], pair[:, LANES:]
            stack = jnp.concatenate([even, left[:, :LANES], other, left[:, LANES:]], axis=0)
            even = jnp.concatenate([even, right[:, :LANES]], axis=0)
            other = jnp.concatenate([other, right[:, LANES:]], axis=0)
            block = jnp.concatenate(
                [
                    jnp.concatenate([even, zero], axis=1),
                    jnp.concatenate([zero, other], axis=1),
                ],
                axis=0,
            )
            moment = lax.dot_general(
                stack, block, (((0,), (0,)), ((), ())), preferred_element_type=jnp.float32
            )
            for side in range(PAIR):
                position = t * PAIR + side
                half = slice(side * LANES, (side + 1) * LANES)
                means[pl.ds(step * size + position, 1), :] = mean[at, half][:, :kept]
                start = (position % 8) * depth
                value = moment[:depth, half] * inverse + eye[...]
                into[position // 8][start : start + depth, :] = value

    def rows_at(step, offset, count):
        at = step * size + offset
        return pl.ds(at if isinstance(at, int) else pl.multiple_of(at, 8), count)

    def copy_out(step, count):
        rows = rows_at(step, 0, count)
        return pltpu.make_async_copy(out.at[rows], cov_ref.at[rows], sems.at[step])

    def rows_out(step, source, count):
        for part, gram in enumerate(source):
            rows = rows_at(step, part * 8, 8)
            for k in range(kept):
                value = gram[pl.ds(k, 8, stride=depth), :]
                out[rows, k * kept : (k + 1) * kept] = value[:, :kept]
        copy_out(step, count).start()

    ready, coming = grams[: len(grams) // 2], grams[len(grams) // 2 :]
    tail = block - (steps - 1) * size
    products(0, ready)

    def two_steps(i, carry):
        products(2 * i + 1, coming)
        rows_out(2 * i, ready, size)
        products(2 * i + 2, ready)
        rows_out(2 * i + 1, coming, size)
        return carry

    lax.fori_loop(0, (steps - 1) // 2, two_steps, 0)
    if steps % 2 == 0:
        products(steps - 1, coming)
        rows_out(steps - 2, ready, size)
        ready = coming
    rows_out(steps - 1, ready, tail)
    mean_ref[...] = means[:block, :]
    for step in range(steps):
        copy_out(step, size if step < steps - 1 else tail).wait()


def shift_tables(h1, h2, h3, owners, group, pitch2, pitch3):
    rows2 = pitch2 * PAIR
    p1 = np.zeros((PAIR, group * rows2, group * h1 * PAIR), np.float32)
    p2 = np.zeros((group * rows2, group * h2 * PAIR), np.float32)
    for y in range(group):
        for x in range(h2):
            for i in range(PAIR):
                to = y * rows2 + x * PAIR + i
                for t in range(PAIR):
                    p1[t, to, (y * h1 + 2 * x + t) * PAIR + i] = 1
                p2[to, (y * h2 + x) * PAIR + i] = 1
    p3 = np.zeros((h3 * pitch3 * PAIR, h3 * h3 * PAIR), np.float32)
    for y in range(h3):
        for x in range(h3):
            for i in range(PAIR):
                p3[(y * pitch3 + x) * PAIR + i, (y * h3 + x) * PAIR + i] = 1
    up = np.zeros((h2 * rows2, h3 * pitch3 * PAIR), np.float32)
    for y in range(h2):
        for x in range(h2):
            for i in range(PAIR):
                up[y * rows2 + x * PAIR + i, ((y // 2) * pitch3 + x // 2) * PAIR + i] = 1
    lines = h1 // owners
    packed = pack_rows(h1, owners)
    c1 = np.zeros((packed, lines * rows2), np.float32)
    c2 = np.zeros((packed, PAIR * rows2), np.float32)
    for x in range(h2):
        for i in range(PAIR):
            for y in range(lines):
                c1[(y * h2 + x) * PAIR + i, y * rows2 + x * PAIR + i] = 1
            for y in range(PAIR):
                c2[((lines + y) * h2 + x) * PAIR + i, y * rows2 + x * PAIR + i] = 1
    small = small_rows(h1, owners)
    half = h2 // PAIR
    ahead = h2 + half
    k1 = np.zeros((PAIR, small, lines * rows2), np.float32)
    k2 = np.zeros((small, rows2), np.float32)
    k3 = np.zeros((small, pitch3 * PAIR), np.float32)
    for i in range(PAIR):
        for x in range(half):
            for y in range(lines):
                for q in range(PAIR):
                    k1[q, (ahead + y * half + x) * PAIR + i, y * rows2 + (PAIR * x + q) * PAIR + i] = 1
            k3[(h2 + x) * PAIR + i, x * PAIR + i] = 1
        for x in range(h2):
            k2[x * PAIR + i, x * PAIR + i] = 1
    tables = []
    p1, k1 = p1.reshape(-1, p1.shape[-1]), k1.reshape(-1, k1.shape[-1])
    for a in (p1, p2, p3, up, c1, c2, k1, k2, k3):
        room = [(0, 0)] * (a.ndim - 1) + [(0, -a.shape[-1] % LANES)]
        tables.append(jnp.asarray(np.pad(a, room), jnp.bfloat16))
    return tables


def pack_rows(h1, owners):
    lines = h1 // owners
    rows = (lines + PAIR) * (h1 // 2) * PAIR
    return -(-rows // 16) * 16


def small_rows(h1, owners):
    half = h1 // 4
    rows = (h1 // owners * half + 3 * half) * PAIR
    return -(-rows // 16) * 16


def packed_path(
    section_one,
    section_two,
    section_three,
    weight_one,
    weight_two,
    weight_three,
    gain_one,
    gain_two,
    gain_three,
    bias_one,
    bias_two,
    bias_three,
    channel_index,
    valid_count,
):
    slots, h1 = section_one.shape[:2]
    h2, h3 = section_two.shape[1], section_three.shape[1]
    c1, c2, c3 = section_one.shape[3], section_two.shape[3], section_three.shape[3]
    kept = channel_index.shape[0]
    owners = lax.axis_size("pos")
    groups = lax.axis_size("img")
    group, pitch2, pitch3 = 4, 16, 8
    tables = shift_tables(h1, h2, h3, owners, group, pitch2, pitch3)
    packed = pack_rows(h1, owners)
    rows2, rows3 = pitch2 * PAIR, pitch3 * PAIR

    def flat(section):
        return jnp.transpose(section, (1, 2, 0, 3)).reshape(-1, section.shape[3])

    index = channel_index.reshape(1, kept)
    smem = pl.BlockSpec(memory_space=pltpu.SMEM)
    vmem = pl.BlockSpec(memory_space=pltpu.VMEM)
    third = jnp.transpose(section_three, (1, 2, 0, 3))
    p1, p2, p3, up, *packing = tables
    operands = [
        *(flat(section_one), p1, weight_one, gain_one.reshape(1, c1), bias_one.reshape(1, c1)),
        index,
        *(flat(section_two), p2, weight_two, gain_two.reshape(1, c2), bias_two.reshape(1, c2)),
        *(third, p3, weight_three, gain_three.reshape(1, c3), bias_three.reshape(1, c3)),
        *(up, *packing),
    ]
    top = small_rows(h1, owners)
    shapes = [(top, LANES)] * owners + [(packed - top, LANES)] * owners
    *packs, small = pl.pallas_call(
        functools.partial(features_kernel, (h1, h2, h3, owners, kept, group, pitch2, pitch3)),
        out_shape=[jax.ShapeDtypeStruct(s, jnp.bfloat16) for s in shapes]
        + [jax.ShapeDtypeStruct((1, 1), jnp.int32)],
        in_specs=[pl.BlockSpec(memory_space=pl.ANY)] * len(operands) + [smem],
        out_specs=[pl.BlockSpec(s, lambda: (0, 0)) for s in shapes] + [smem],
        scratch_shapes=[
            pltpu.VMEM(((h1 + 2) * rows2, 2 * LANES), jnp.bfloat16),
            pltpu.VMEM(((h2 + 2) * rows2, 3 * LANES), jnp.bfloat16),
            pltpu.VMEM(((h3 + 2) * rows3, 3 * c3), jnp.bfloat16),
            pltpu.VMEM((h3 * h3 * PAIR, c3), jnp.bfloat16),
            pltpu.VMEM((3, 2 * LANES, LANES), jnp.bfloat16),
            pltpu.VMEM((h1 * rows2, LANES), jnp.bfloat16),
            pltpu.VMEM((h2 * rows2, LANES), jnp.bfloat16),
            pltpu.VMEM((h3 * rows3, c3), jnp.bfloat16),
            pltpu.VMEM((h1 * rows2, LANES), jnp.bfloat16),
            pltpu.VMEM((h2 * rows2, LANES), jnp.bfloat16),
            pltpu.VMEM(((h3 + 1) * rows3, LANES), jnp.bfloat16),
            pltpu.SemaphoreType.DMA((len(operands),)),
        ]
        + [pltpu.VMEM(a.shape, a.dtype) for a in operands],
        name="features",
    )(*operands, valid_count)
    sizes = (slots, h1, h2, kept, owners, groups)

    def small_packs(index, *packs):
        return finish(sizes, True, index, packs[:owners])

    def large_packs(index, *packs):
        full = [jnp.concatenate(p, axis=0) for p in zip(packs[:owners], packs[owners:])]
        return finish(sizes, False, index, full)

    mean, covariance = lax.cond(small[0, 0] > 0, small_packs, large_packs, index, *packs)
    return mean.T, covariance


def finish(sizes, small, index, packs):
    slots, h1, h2, kept, owners, groups = sizes
    packed = packs[0].shape[0]
    vmem = pl.BlockSpec(memory_space=pltpu.VMEM)

    parts = [packs[0]]
    for k in range(1, owners):
        pairs = [(i, i ^ k) for i in range(owners)]
        parts.append(lax.ppermute(packs[k], "pos", pairs))
    merged = pl.pallas_call(
        merge_kernel,
        out_shape=jax.ShapeDtypeStruct((packed * owners, LANES), jnp.bfloat16),
        in_specs=[vmem] * owners,
        out_specs=vmem,
        compiler_params=pltpu.CompilerParams(vmem_limit_bytes=8 << 20),
        name="merge",
    )(*parts)

    levels = groups // PAIR
    shards = [merged]
    turns = sorted(range(1, levels), key=lambda t: (min(t, levels - t), t))
    for turn in turns:
        pairs = [
            (z * PAIR + c, ((z + turn) % levels) * PAIR + c)
            for z in range(levels)
            for c in range(PAIR)
        ]
        shards.append(lax.ppermute(merged, "img", pairs))
    swap = [(i, i ^ 1) for i in range(groups)]
    shards = shards + [lax.ppermute(s, "img", swap) for s in shards]

    lines, columns = h1 // owners, h2
    block = lines * h1
    each = owners * slots
    images = each * len(shards)
    shards = [s.reshape(packed // PAIR, each, LANES) for s in shards]
    parts = 2
    size = 8 * parts
    steps = -(-block // size)
    depth = -(-(kept + 1) // 8) * 8
    return pl.pallas_call(
        functools.partial(
            covariance_kernel, (len(shards), lines, columns, kept, depth, size // PAIR, small)
        ),
        out_shape=(
            jax.ShapeDtypeStruct((block, kept), jnp.float32),
            jax.ShapeDtypeStruct((block, kept * kept), jnp.float32),
        ),
        in_specs=[vmem] * (1 + len(shards)),
        out_specs=(vmem, pl.BlockSpec(memory_space=pl.ANY)),
        compiler_params=pltpu.CompilerParams(vmem_limit_bytes=24 << 20),
        scratch_shapes=[
            pltpu.VMEM((packed // PAIR, images, LANES), jnp.bfloat16),
            pltpu.VMEM((size // PAIR * images, 2 * LANES), jnp.bfloat16),
            pltpu.VMEM(((1 if small else 2) * LANES, 2 * LANES), jnp.bfloat16),
            pltpu.VMEM((depth, LANES), jnp.float32),
            pltpu.VMEM((steps * size, kept), jnp.float32),
            pltpu.VMEM((steps * size, kept * kept), jnp.float32),
            pltpu.SemaphoreType.DMA((steps,)),
            pltpu.VMEM((4 * columns, images, LANES), jnp.bfloat16),
        ]
        + [pltpu.VMEM((8 * depth, LANES), jnp.float32) for _ in range(2 * parts)],
        name="covariance",
    )(index, *shards)


def suits(mesh, section_one, section_two, section_three, channel_index):
    owners, groups = mesh.shape["pos"], mesh.shape["img"]
    devices = owners * groups
    images, h1, _, c1 = section_one.shape
    h2, c2 = section_two.shape[1], section_two.shape[3]
    h3, c3 = section_three.shape[1], section_three.shape[3]
    kept = channel_index.shape[0]
    lines = h1 // owners
    return (
        images == PAIR * devices
        and owners == 4
        and groups % PAIR == 0
        and h1 % owners == 0
        and h1 == 2 * h2 == 4 * h3
        and h2 <= 16
        and h3 <= 8
        and (c1, c2, c3) == (HALF, LANES, 2 * LANES)
        and HALF <= kept < LANES
        and kept - HALF < THIRD
        and lines == 7
    )


def solution(mesh):
    in_specs = (
        P(("img", "pos"), None, None, None),
        P(("img", "pos"), None, None, None),
        P(("img", "pos"), None, None, None),
        P(),
        P(),
        P(),
        P(),
        P(),
        P(),
        P(),
        P(),
        P(),
        P(),
        P("img", "pos"),
    )

    def run(*arrays):
        chosen = suits(mesh, arrays[0], arrays[1], arrays[2], arrays[12])
        return jax.shard_map(
            packed_path if chosen else plain,
            mesh=mesh,
            in_specs=in_specs,
            out_specs=(P(None, "pos"), P("pos", None)),
            check_vma=False,
        )(*arrays)

    return run
```
